32 devices in a mesh: gx: 8 (over z, core), gy: 2 (over y), gz: 2 (over x).
Axes of the slice: x: 2, y: 2, z: 4, core: 2. Of those that a mesh axis runs over, the one named last changes fastest.
Arguments:
- adjoint: float32 [2, 4, 16, 64, 256], P(None, None, 'gz', 'gx', 'gy'), may hold values from -6 to 6
- saved_state: float32 [4, 4, 16, 64, 256], P(None, None, 'gz', 'gx', 'gy'), may hold values from -6 to 6
- wind_field: float32 [3, 16, 64, 256], P(None, 'gz', 'gx', 'gy'), may hold values from -0.3 to 0.3
- facade_slot: int32 [16, 64, 256], P('gz', 'gx', 'gy'), may hold values from 0 to 64, as said below
- facade_table: int32 [2, 8, 2, 64], P('gz', 'gx', 'gy'), may hold values from 0 to 1023, as said below
- impedance: float32 [1024], replicated, may hold values from 0.1 to 1
Outputs:
- adjoint_out: float32 [2, 4, 16, 64, 256], P(None, None, 'gz', 'gx', 'gy')
- gradient: float32 [1024], P(('gx', 'gy', 'gz'))
The draws below stay inside these ranges and needn't reach their ends.
Inputs may be any that keep to these rules, and one draw needn't show every extreme that they name: `facade_slot`: slots name entries of the cell's own device block table. `facade_table`: A block's facades are owned by that block's device or by one of the two devices beside it along gx (wrapping), the owner of facade f being the device of index f // 32 along gx+gy+gz; ids may repeat within and across tables.
All inputs are finite; a program needn't handle non-finite values.
Results may differ from the reference program's by a relative error of at most 0.00013.
Values sent between devices are 32-bit elements; how exact they have to be, the bound alone decides.
No kernel may reach another device: no remote copies, remote signals or barrier semaphores. Data moves between devices by JAX's collectives and lax.ppermute only.
A program may use at most 64 MiB of HBM per device.

```python
import math
import jax
import jax.numpy as jnp

CX = 8
CY = 128
CZ = 8
STEPS = 4
LOC = 64
FAC_DEV = 32
NX = 64
NY = 256
NZ = 16
FACADES = 1024


def draw_facade_slot(key, part):
    key_level, key_cell, key_slot = jax.random.split(key, 3)
    level = jax.random.randint(key_level, (NZ // CZ, NX // CX, NY // CY), 0, 4)
    density = jnp.left_shift(jnp.int32(1), level.astype(jnp.int32))
    cell_density = jnp.repeat(jnp.repeat(jnp.repeat(density, CZ, axis=0), CX, axis=1), CY, axis=2)
    on_facade = jax.random.randint(key_cell, (NZ, NX, NY), 0, 16) < cell_density
    slot_of = jax.random.randint(key_slot, (NZ, NX, NY), 1, LOC + 1)
    result = jnp.where(on_facade, slot_of, 0)
    result = result.at[0, 0, 0].set(LOC).at[0, 0, 1].set(0)
    return result.astype(jnp.int32)


def draw_facade_table(key, part):
    key_offset, key_name = jax.random.split(jax.random.fold_in(key, 7), 2)
    blocks_z = NZ // CZ
    blocks_x = NX // CX
    blocks_y = NY // CY
    shape = (blocks_z, blocks_x, blocks_y, LOC)
    offset = jax.random.randint(key_offset, shape, -1, 2)
    block_z = jnp.arange(blocks_z, dtype=jnp.int32)[:, None, None, None]
    block_x = jnp.arange(blocks_x, dtype=jnp.int32)[None, :, None, None]
    block_y = jnp.arange(blocks_y, dtype=jnp.int32)[None, None, :, None]
    owner_x = (block_x + offset + blocks_x) % blocks_x
    owner_block = (owner_x * blocks_y + block_y) * blocks_z + block_z
    result = owner_block * FAC_DEV + jax.random.randint(key_name, shape, 0, FAC_DEV)
    total = FAC_DEV * blocks_z * blocks_x * blocks_y
    result = result.at[0, 0, 0, 0].set(0).at[blocks_z - 1, blocks_x - 1, blocks_y - 1, LOC - 1].set(total - 1)
    return result.astype(jnp.int32)


def levels(rng, extent, cuts, least, largest):
    def one(dim, shards_of):
        heights = jax.random.uniform(jax.random.fold_in(jax.random.fold_in(rng, 6), dim), (shards_of,), jnp.float32, least / len(cuts), largest / len(cuts))
        return jnp.repeat(jnp.exp(heights), extent[dim] // shards_of).reshape((-1,) + (1,) * (len(extent) - dim - 1))

    gain = one(*cuts[0])
    for cut in cuts[1:]:
        gain = gain * one(*cut)
    return gain


def normal_values(key, extent, scale, most, cuts=(), kind=jnp.bfloat16):
    array = jax.random.normal(key, extent, jnp.float32) * scale
    if len(cuts) > 0:
        array = levels(key, extent, cuts, -0.22, 0.18) * array
    return jnp.clip(array, min=-most, max=most).astype(kind)


def setup_inputs(seed: int = 0) -> dict:
    streams_of = jax.random.split(jax.random.key(seed), 7)
    return {
        "adjoint": normal_values(streams_of[0], (2, 4, NZ, NX, NY), 1.0, 6.0, ((2, 2), (3, 8), (4, 2)), jnp.float32),
        "saved_state": normal_values(streams_of[1], (STEPS, 4, NZ, NX, NY), 1.0, 6.0, ((2, 2), (3, 8), (4, 2)), jnp.float32),
        "wind_field": jnp.clip(jax.random.uniform(streams_of[2], (3, NZ, NX, NY), jnp.float32, -0.3, 0.3) * levels(streams_of[2], (3, NZ, NX, NY), ((1, 2), (2, 8), (3, 2)), -0.4, 0.0), -0.3, 0.3),
        "facade_slot": draw_facade_slot(jax.random.fold_in(streams_of[6], 71), 0),
        "facade_table": draw_facade_table(jax.random.fold_in(streams_of[6], 71), 0),
        "impedance": jnp.clip(jnp.exp(jax.random.uniform(streams_of[5], (FACADES,), jnp.float32, math.log(0.1), math.log(1.0))), 0.1, 1.0),
    }


TIME_STEP = 0.3


def trimmed(field, axis_k, offset):
    selector = [slice(None)] * field.ndim
    for j in range(3):
        dim = field.ndim - 3 + j
        length = field.shape[dim]
        if j == axis_k:
            selector[dim] = slice(1 + offset, length - 1 + offset)
        else:
            selector[dim] = slice(1, length - 1)
    return field[tuple(selector)]


def interior(field):
    return trimmed(field, 0, 0)


def central_diff(field, axis_k):
    return 0.5 * (trimmed(field, axis_k, 1) - trimmed(field, axis_k, -1))


def tendency(state_pad, wind_pad, damping_pad):
    pressure = state_pad[0]
    damping = interior(damping_pad)
    result = []
    for index in range(4):
        component = state_pad[index]
        advection = central_diff(wind_pad[0] * component, 0) + central_diff(wind_pad[1] * component, 1) + central_diff(wind_pad[2] * component, 2)
        if index == 0:
            coupling = central_diff(state_pad[1], 0) + central_diff(state_pad[2], 1) + central_diff(state_pad[3], 2)
        else:
            coupling = central_diff(pressure, index - 1)
        result.append(advection + coupling - damping * interior(component))
    return jnp.stack(result)


def padded_one(field):
    return jnp.pad(field, [(0, 0)] * (field.ndim - 3) + [(1, 1)] * 3)


def reference(adjoint, saved_state, wind_field, facade_slot, facade_table, impedance):
    blocks_x = NX // CX
    blocks_y = NY // CY
    block_z = (jnp.arange(NZ, dtype=jnp.int32) // CZ)[:, None, None]
    block_x = (jnp.arange(NX, dtype=jnp.int32) // CX)[None, :, None]
    block_y = (jnp.arange(NY, dtype=jnp.int32) // CY)[None, None, :]
    on_facade = facade_slot > 0
    flat_index = ((block_z * blocks_x + block_x) * blocks_y + block_y) * LOC + jnp.maximum(facade_slot - 1, 0)
    facade_of = facade_table.reshape(-1)[flat_index.astype(jnp.int32)]
    damping = jnp.where(on_facade, impedance[facade_of], jnp.float32(0.0))
    wind_pad = padded_one(wind_field)
    damping_pad = padded_one(damping)
    upper = adjoint[0]
    middle = adjoint[1]
    products = jnp.zeros((NZ, NX, NY), jnp.float32)
    for step in range(STEPS):
        products = products + jnp.sum(middle * saved_state[step], axis=0)
        newest = upper + 2.0 * TIME_STEP * tendency(padded_one(middle), wind_pad, damping_pad)
        upper, middle = middle, newest
    terms = jnp.where(on_facade, -2.0 * TIME_STEP * products, jnp.float32(0.0)).reshape(-1)
    owners = jnp.where(on_facade, facade_of, 0).reshape(-1).astype(jnp.int32)
    gradient = jax.ops.segment_sum(terms, owners, num_segments=FACADES)
    return jnp.stack([upper, middle]), gradient
```

```python
import functools

import jax
import jax.numpy as jnp
from jax import lax
from jax.experimental import pallas as pl
from jax.experimental.pallas import tpu as pltpu
from jax.sharding import PartitionSpec as P

FAC_DEV = 32
TIME_STEP = 0.3
SCALE = 2.0 * TIME_STEP

FIELDS = 12
DEPTH = 4
Z_PLANES = [(f, t) for t in (1, 2, 3) for f in range(FIELDS)] + [(f, 4) for f in (0, 1, 2, 3, 8)]
D_PLANES = [(f, t) for t in (1, 2) for f in range(FIELDS)] + [(f, 3) for f in (0, 1, 2, 3, 8, 10)]
E_PLANES = [(f, t) for t in (1, 2) for f in range(FIELDS)] + [(f, 3) for f in (0, 1, 2, 3, 8, 9)]
GROUPS = 32


def z_of(s, depth_z):
    return jnp.where(lax.axis_index("gz") == 0, depth_z - 1 - s, s)


def own_planes(depth_z):
    return [(f, s) for f in range(FIELDS) for s in range(depth_z)]


def lane_iota():
    return lax.broadcasted_iota(jnp.int32, (8, 128), 1)


def row_iota():
    return lax.broadcasted_iota(jnp.int32, (8, 128), 0)


def pack_lanes(load, planes, send_high):
    lanes = lane_iota() // DEPTH
    packed = []
    for start in range(0, len(planes), GROUPS):
        row = jnp.zeros((8, 128), jnp.float32)
        for j, plane in enumerate(planes[start:start + GROUPS]):
            shift = lax.rem(DEPTH * j + jnp.where(send_high, DEPTH, 0), 128)
            row = jnp.where(lanes == j, pltpu.roll(load(*plane), shift, 1), row)
        packed.append(row)
    return packed


def pack_rows(first, second, send_high, rows):
    turned = pltpu.roll(second, 4, 0)
    low = jnp.where(rows < 4, first, turned)
    high = jnp.where(rows < 4, turned, first)
    return jnp.where(send_high, high, low)


def unpack_rows(got_a, got_b, even, rows):
    from_high = jnp.where(even, got_a, got_b)
    from_low = jnp.where(even, got_b, got_a)
    first = jnp.where(rows < 4, from_high, from_low)
    second = pltpu.roll(jnp.where(rows < 4, from_low, from_high), 4, 0)
    return first, second


def owner_of(offset):
    count_x, count_y, count_z = (lax.axis_size(a) for a in ("gx", "gy", "gz"))
    x = lax.rem(lax.axis_index("gx") + (offset + count_x), count_x)
    return (x * count_y + lax.axis_index("gy")) * count_z + lax.axis_index("gz")


def pack_kernel(sides, adjoint, wind, slots, table, impedance, *outs):
    damping, zb = outs[:2]
    ys = outs[2:2 + sides]
    ds = outs[2 + sides:2 + 2 * sides]
    xa, xb = outs[2 + 2 * sides:4 + 2 * sides]
    names = outs[4 + 2 * sides]
    depth_z = slots.shape[0]
    names[...] = jnp.zeros((8, 128), jnp.int32)
    names[:, :table.shape[1]] = jnp.broadcast_to(table[...], (8, table.shape[1]))
    ids = names[...]
    local = jnp.zeros((8, 128), jnp.float32)
    for offset in (-1, 0, 1):
        row = owner_of(offset) * FAC_DEV // 128
        values = jnp.broadcast_to(impedance[pl.ds(row, 1), :], (8, 128))
        local = jnp.where(ids // 128 == row, jnp.take_along_axis(values, ids % 128, axis=1), local)
    for z in range(depth_z):
        slot = slots[z]
        found = jnp.take_along_axis(local, jnp.maximum(slot - 1, 0), axis=1)
        damping[z] = jnp.where(slot > 0, found, 0.0)

    def load(f, s):
        z = z_of(s, depth_z)
        if f < 4:
            return adjoint[1, f, z]
        if f < 8:
            return adjoint[0, f - 4, z]
        if f < 11:
            return wind[f - 8, z]
        return damping[z]

    for i, (f, t) in enumerate(Z_PLANES):
        zb[i] = load(f, t - 1)
    even_y = lax.rem(lax.axis_index("gy"), 2) == 0
    for side in range(sides):
        send_high = even_y if side == 0 else jnp.logical_not(even_y)
        for i, row in enumerate(pack_lanes(load, own_planes(depth_z), send_high)):
            ys[side][i] = row
        for i, row in enumerate(pack_lanes(lambda f, t: load(f, t - 1), D_PLANES, send_high)):
            ds[side][i] = row
    even_x = lax.rem(lax.axis_index("gx"), 2) == 0
    rows = row_iota()
    planes = own_planes(depth_z)
    for i in range(len(planes) // 2):
        first, second = load(*planes[2 * i]), load(*planes[2 * i + 1])
        xa[i] = pack_rows(first, second, even_x, rows)
        xb[i] = pack_rows(first, second, jnp.logical_not(even_x), rows)


def edge_kernel(sides, zb, *rest):
    ys = rest[:sides]
    ds = rest[sides:2 * sides]
    xa, xb = rest[2 * sides:]
    loads = [functools.partial(lambda i: zb[i], Z_PLANES.index(p)) for p in E_PLANES]
    for ref in ys + ds:
        loads += [functools.partial(lambda ref, i: ref[i], ref, i) for i in range(ref.shape[0])]
    even_x = lax.rem(lax.axis_index("gx"), 2) == 0
    rows = row_iota()
    for i in range(len(loads) // 2):
        first, second = loads[2 * i](), loads[2 * i + 1]()
        xa[i] = pack_rows(first, second, even_x, rows)
        xb[i] = pack_rows(first, second, jnp.logical_not(even_x), rows)


def coupled(middle, c, k):
    if c == 0:
        return middle[1 + k]
    if c == 1 + k:
        return middle[0]
    return None


def flux(wind, middle, c, k):
    value = wind * middle[c]
    other = coupled(middle, c, k)
    return value if other is None else value + other


def step_kernel(sides, adjoint, wind, damping, saved, slots, table, zb, *rest):
    ys = rest[:sides]
    ds = rest[sides:2 * sides]
    oa, ob, ea, eb, out, own, part_a, part_b, cells, prod, acc = rest[2 * sides:]
    depth_z = slots.shape[0]
    rows, lanes = row_iota(), lane_iota()
    even_x = lax.rem(lax.axis_index("gx"), 2) == 0
    even_y = lax.rem(lax.axis_index("gy"), 2) == 0
    zero = jnp.zeros((8, 128), jnp.float32)
    far = DEPTH + depth_z

    def put(f, slot, tx, ty, value):
        cells[f, slot, 8 * tx:8 * tx + 8, 128 * ty:128 * ty + 128] = value

    for s in range(depth_z):
        z = z_of(s, depth_z)
        for f in range(4):
            put(f, DEPTH + s, 0, 0, adjoint[1, f, z])
            put(4 + f, DEPTH + s, 0, 0, adjoint[0, f, z])
        for f in range(3):
            put(8 + f, DEPTH + s, 0, 0, wind[f, z])
        put(11, DEPTH + s, 0, 0, damping[z])
    for i, (f, t) in enumerate(Z_PLANES):
        put(f, DEPTH - t, 0, 0, zb[i])
    planes = own_planes(depth_z)
    for i in range(len(planes) // 2):
        pair = unpack_rows(oa[i], ob[i], even_x, rows)
        for (f, s), value in zip(planes[2 * i:2 * i + 2], pair):
            put(f, DEPTH + s, 1, 0, value)
    edges = []
    for i in range(ea.shape[0]):
        edges += unpack_rows(ea[i], eb[i], even_x, rows)
    for (f, t), value in zip(E_PLANES, edges):
        put(f, DEPTH - t, 1, 0, value)
    edges = edges[len(E_PLANES):]
    packs = [ref[i] for ref in ys + ds for i in range(ref.shape[0])]
    y_rows = ys[0].shape[0]

    def spread(packed, j, side):
        high = even_y if side == 0 else jnp.logical_not(even_y)
        shift = lax.rem(256 - DEPTH * j - jnp.where(high, 0, DEPTH), 128)
        start = jnp.where(high, 0, 128 - DEPTH)
        return jnp.where((lanes >= start) & (lanes < start + DEPTH), pltpu.roll(packed, shift, 1), 0.0)

    def spread_all(index, j):
        for tx, source in ((0, packs), (1, edges)):
            value = spread(source[index(0)], j, 0)
            if sides > 1:
                value = value + spread(source[index(1)], j, 1)
            yield tx, value

    for i, (f, s) in enumerate(planes):
        for tx, value in spread_all(lambda side: side * y_rows + i // GROUPS, i % GROUPS):
            put(f, DEPTH + s, tx, 1, value)
    for i, (f, t) in enumerate(D_PLANES):
        for tx, value in spread_all(lambda side: sides * y_rows + side, i):
            put(f, DEPTH - t, tx, 1, value)
    for tx in range(2):
        for ty in range(2):
            for f in range(9):
                put(f, far, tx, ty, zero)
            if tx + ty:
                for f in (0, 1, 2, 3, 8):
                    put(f, 0, tx, ty, zero)
                for f in (4, 5, 6, 7, 9, 10, 11):
                    if not (f == 9 and ty == 0) and not (f == 10 and ty == 1):
                        put(f, 1, tx, ty, zero)

    grid_row = lax.broadcasted_iota(jnp.int32, (16, 256), 0)
    grid_lane = lax.broadcasted_iota(jnp.int32, (16, 256), 1)
    x, y = lax.axis_index("gx"), lax.axis_index("gy")
    row_end = jnp.where(x == lax.axis_size("gx") - 1, 8, 12)
    row_restart = jnp.where(x == 0, 16, 12)
    lane_end = jnp.where(y == lax.axis_size("gy") - 1, 128, 192)
    lane_restart = jnp.where(y == 0, 256, 192)
    inside = (grid_row < row_end) | (grid_row >= row_restart)
    inside &= (grid_lane < lane_end) | (grid_lane >= lane_restart)
    factor = jnp.where(inside, jnp.float32(0.5 * SCALE), 0.0)
    sign = jnp.where(lax.axis_index("gz") == 0, jnp.float32(-1.0), jnp.float32(1.0))

    def full_step(first, middle_at, upper_at):
        def body(slot, carry):
            middle = [cells[middle_at + c, slot] for c in range(4)]
            above = [cells[middle_at + c, slot + 1] for c in range(4)]
            below = [cells[middle_at + c, slot - 1] for c in range(4)]
            wind_up, wind_down = cells[8, slot + 1], cells[8, slot - 1]
            wind_x, wind_y = cells[9, slot], cells[10, slot]
            loss = SCALE * cells[11, slot]
            for c in range(4):
                total = sign * (flux(wind_up, above, c, 0) - flux(wind_down, below, c, 0))
                along = flux(wind_x, middle, c, 1)
                total += pltpu.roll(along, 15, 0) - pltpu.roll(along, 1, 0)
                along = flux(wind_y, middle, c, 2)
                total += pltpu.roll(along, 255, 1) - pltpu.roll(along, 1, 1)
                cells[upper_at + c, slot] = cells[upper_at + c, slot] + factor * total - loss * middle[c]
            return carry

        lax.fori_loop(first, far, body, 0)

    def last_step(middle_at, upper_at):
        def body(s, carry):
            slot = DEPTH + s
            own_part = (slice(0, 8), slice(0, 128))
            middle = [cells[(middle_at + c, slot) + own_part] for c in range(4)]
            above = [cells[(middle_at + c, slot + 1) + own_part] for c in range(4)]
            below = [cells[(middle_at + c, slot - 1) + own_part] for c in range(4)]
            mid_x = [cells[middle_at + c, slot, :, 0:128] for c in range(4)]
            mid_y = [cells[middle_at + c, slot, 0:8, :] for c in range(4)]
            wind_up, wind_down = cells[(8, slot + 1) + own_part], cells[(8, slot - 1) + own_part]
            wind_x, wind_y = cells[9, slot, :, 0:128], cells[10, slot, 0:8, :]
            loss = SCALE * cells[(11, slot) + own_part]
            z = z_of(s, depth_z)
            for c in range(4):
                total = sign * (flux(wind_up, above, c, 0) - flux(wind_down, below, c, 0))
                along = flux(wind_x, mid_x, c, 1)
                total += (pltpu.roll(along, 15, 0) - pltpu.roll(along, 1, 0))[0:8]
                along = flux(wind_y, mid_y, c, 2)
                total += (pltpu.roll(along, 255, 1) - pltpu.roll(along, 1, 1))[:, 0:128]
                upper = cells[(upper_at + c, slot) + own_part]
                out[0, c, z] = middle[c]
                out[1, c, z] = upper + jnp.float32(0.5 * SCALE) * total - loss * middle[c]
            return carry

        lax.fori_loop(0, depth_z, body, 0)

    def products(step, middle_at, slot, z):
        return sum(cells[middle_at + c, slot, 0:8, 0:128] * saved[step, c, z] for c in range(4))

    full_step(1, 0, 4)
    for s in range(depth_z):
        z = z_of(s, depth_z)
        prod[z] = products(0, 0, DEPTH + s, z) + products(1, 4, DEPTH + s, z)
    full_step(2, 4, 0)
    full_step(3, 0, 4)
    for s in range(depth_z):
        z = z_of(s, depth_z)
        prod[z] = -SCALE * (prod[z] + (products(2, 0, DEPTH + s, z) + products(3, 4, DEPTH + s, z)))
    last_step(4, 0)

    slot_count = table.shape[1]
    level = lax.broadcasted_iota(jnp.int32, (slot_count, 128), 0) + 1
    acc[...] = jnp.zeros((slot_count, 128), jnp.float32)

    def by_slot(z, carry):
        total = acc[...]
        for row in range(8):
            cell_slot = jnp.broadcast_to(slots[z, row:row + 1, :], (slot_count, 128))
            term = jnp.broadcast_to(prod[z, row:row + 1, :], (slot_count, 128))
            total = total + jnp.where(cell_slot == level, term, 0.0)
        acc[...] = total
        return carry

    lax.fori_loop(0, depth_z, by_slot, 0)
    slot_terms = jnp.sum(acc[...], axis=1, keepdims=True)
    names = jnp.broadcast_to(table[...], (slot_count, slot_count))
    diagonal = lax.broadcasted_iota(jnp.int32, (slot_count, slot_count), 0) == lax.broadcasted_iota(
        jnp.int32, (slot_count, slot_count), 1
    )
    column = jnp.sum(jnp.where(diagonal, names, 0).astype(jnp.float32), axis=1, keepdims=True)
    lane = lax.broadcasted_iota(jnp.int32, (slot_count, 128), 1)

    def bucket(offset):
        target = jnp.where(lane < FAC_DEV, owner_of(offset) * FAC_DEV + lane, -1).astype(jnp.float32)
        return jnp.sum(jnp.where(column == target, slot_terms, 0.0), axis=0, keepdims=True)

    upward, downward = bucket(1), bucket(-1)
    own[...] = bucket(0)
    part_a[...] = jnp.where(even_x, upward, downward)
    part_b[...] = jnp.where(even_x, downward, upward)


def swap_a(block, axis):
    return lax.ppermute(block, axis, [(i, i ^ 1) for i in range(lax.axis_size(axis))])


def swap_b(block, axis, wrap=False):
    count = lax.axis_size(axis)
    pairs = [(i, (i + 1 if i % 2 else i - 1) % count) for i in range(count)]
    if not wrap:
        pairs = pairs[1:-1]
    return lax.ppermute(block, axis, pairs)


def swap_diagonal(block, side):
    count_y, count_z = lax.axis_size("gy"), lax.axis_size("gz")
    pairs = []
    for y in range(count_y):
        step = 1 if (y % 2 == 0) == (side == 0) else -1
        if 0 <= y + step < count_y:
            pairs += [(y * count_z + z, (y + step) * count_z + (z ^ 1)) for z in range(count_z)]
    return lax.ppermute(block, ("gy", "gz"), pairs)


def vmem(count):
    return [pl.BlockSpec(memory_space=pltpu.VMEM)] * count


def rows_of(count):
    return jax.ShapeDtypeStruct((count, 8, 128), jnp.float32)


def local(adjoint, saved_state, wind_field, facade_slot, facade_table, impedance):
    depth_z = facade_slot.shape[0]
    sides = 1 if lax.axis_size("gy") == 2 else 2
    table = facade_table.reshape(1, -1)
    rates = impedance.reshape(-1, 128)
    own_count = FIELDS * depth_z
    y_rows = -(-own_count // GROUPS)
    packed = pl.pallas_call(
        functools.partial(pack_kernel, sides),
        out_shape=[rows_of(depth_z), rows_of(len(Z_PLANES))]
        + [rows_of(y_rows)] * sides
        + [rows_of(1)] * sides
        + [rows_of(own_count // 2)] * 2,
        in_specs=vmem(5),
        out_specs=vmem(4 + 2 * sides),
        scratch_shapes=[pltpu.VMEM((8, 128), jnp.int32)],
        name="pack",
    )(adjoint, wind_field, facade_slot, table, rates)
    damping, zb = packed[:2]
    ys, ds = packed[2:2 + sides], packed[2 + sides:2 + 2 * sides]
    xa, xb = packed[2 + 2 * sides:]
    with jax.named_scope("z_swap"):
        zb = swap_a(zb, "gz")
    with jax.named_scope("y_swap"):
        ys = [swap_a(b, "gy") if side == 0 else swap_b(b, "gy") for side, b in enumerate(ys)]
    with jax.named_scope("d_swap"):
        ds = [swap_diagonal(b, side) for side, b in enumerate(ds)]
    with jax.named_scope("x_swap"):
        xb = swap_b(xb, "gx")
        xa = swap_a(xa, "gx")
    edge_count = (len(E_PLANES) + sides * (y_rows + 1)) // 2
    ea, eb = pl.pallas_call(
        functools.partial(edge_kernel, sides),
        out_shape=[rows_of(edge_count)] * 2,
        in_specs=vmem(1 + 2 * sides),
        out_specs=vmem(2),
        name="edges",
    )(zb, *ys, *ds)
    with jax.named_scope("e_swap"):
        eb = swap_b(eb, "gx")
        ea = swap_a(ea, "gx")
    slot_count = table.shape[1]
    row = jax.ShapeDtypeStruct((1, 128), jnp.float32)
    out, own, part_a, part_b = pl.pallas_call(
        functools.partial(step_kernel, sides),
        out_shape=[jax.ShapeDtypeStruct(adjoint.shape, jnp.float32), row, row, row],
        in_specs=vmem(11 + 2 * sides),
        out_specs=vmem(4),
        scratch_shapes=[
            pltpu.VMEM((FIELDS, DEPTH + depth_z + 1, 16, 256), jnp.float32),
            pltpu.VMEM((depth_z, 8, 128), jnp.float32),
            pltpu.VMEM((slot_count, 128), jnp.float32),
        ],
        name="steps",
    )(adjoint, wind_field, damping, saved_state, facade_slot, table, zb, *ys, *ds, xa, xb, ea, eb)
    with jax.named_scope("g_swap"):
        part_b = swap_b(part_b, "gx", wrap=True)
        part_a = swap_a(part_a, "gx")
    gradient = (own + part_a + part_b)[0, :FAC_DEV]
    return out, gradient


def solution(mesh):
    return jax.shard_map(
        local,
        mesh=mesh,
        in_specs=(
            P(None, None, "gz", "gx", "gy"),
            P(None, None, "gz", "gx", "gy"),
            P(None, "gz", "gx", "gy"),
            P("gz", "gx", "gy"),
            P("gz", "gx", "gy", None),
            P(),
        ),
        out_specs=(P(None, None, "gz", "gx", "gy"), P(("gx", "gy", "gz"))),
        check_vma=False,
    )
```

```python
import functools

import jax
import jax.numpy as jnp
from jax import lax
from jax.experimental import pallas as pl
from jax.experimental.pallas import tpu as pltpu
from jax.sharding import PartitionSpec as P

FAC_DEV = 32
TIME_STEP = 0.3
SCALE = 2.0 * TIME_STEP

FIELDS = 12
DEPTH = 4
Z_PLANES = [(f, t) for t in (1, 2, 3) for f in range(FIELDS)] + [(f, 4) for f in (0, 1, 2, 3, 8)]
D_PLANES = [(f, t) for t in (1, 2) for f in range(FIELDS)] + [(f, 3) for f in (0, 1, 2, 3, 8, 10)]
E_PLANES = [(f, t) for t in (1, 2) for f in range(FIELDS)] + [(f, 3) for f in (0, 1, 2, 3, 8, 9)]
GROUPS = 32


def z_of(s, depth_z):
    return jnp.where(lax.axis_index("gz") == 0, depth_z - 1 - s, s)


def z_sign():
    return jnp.where(lax.axis_index("gz") == 0, jnp.float32(-1.0), jnp.float32(1.0))


def own_planes(depth_z):
    return [(f, s) for f in range(FIELDS) for s in range(depth_z)]


def lane_iota():
    return lax.broadcasted_iota(jnp.int32, (8, 128), 1)


def row_iota():
    return lax.broadcasted_iota(jnp.int32, (8, 128), 0)


def pack_lanes(load, planes, send_high):
    lanes = lane_iota() // DEPTH
    packed = []
    for start in range(0, len(planes), GROUPS):
        row = jnp.zeros((8, 128), jnp.float32)
        for j, plane in enumerate(planes[start:start + GROUPS]):
            shift = lax.rem(DEPTH * j + jnp.where(send_high, DEPTH, 0), 128)
            row = jnp.where(lanes == j, pltpu.roll(load(*plane), shift, 1), row)
        packed.append(row)
    return packed


def pack_rows(first, second, send_high, rows):
    turned = pltpu.roll(second, 4, 0)
    low = jnp.where(rows < 4, first, turned)
    high = jnp.where(rows < 4, turned, first)
    return jnp.where(send_high, high, low)


def unpack_rows(got_a, got_b, even, rows):
    from_high = jnp.where(even, got_a, got_b)
    from_low = jnp.where(even, got_b, got_a)
    first = jnp.where(rows < 4, from_high, from_low)
    second = pltpu.roll(jnp.where(rows < 4, from_low, from_high), 4, 0)
    return first, second


def owner_of(offset):
    count_x, count_y, count_z = (lax.axis_size(a) for a in ("gx", "gy", "gz"))
    x = lax.rem(lax.axis_index("gx") + (offset + count_x), count_x)
    return (x * count_y + lax.axis_index("gy")) * count_z + lax.axis_index("gz")


def pack_kernel(sides, *refs):
    sources = refs[:5]
    adjoint, wind, slots, table, damping, zb = refs[5:11]
    ys = refs[11:11 + sides]
    ds = refs[11 + sides:11 + 2 * sides]
    xa, xb, impedance, names, sems = refs[11 + 2 * sides:]
    targets = (adjoint, wind, slots, table, impedance)
    copies = [pltpu.make_async_copy(a, b, sems.at[i]) for i, (a, b) in enumerate(zip(sources, targets))]
    for i in (3, 4, 2, 0, 1):
        copies[i].start()
    depth_z = slots.shape[0]
    names[...] = jnp.zeros((8, 128), jnp.int32)
    copies[3].wait()
    names[:, :table.shape[1]] = jnp.broadcast_to(table[...], (8, table.shape[1]))
    copies[4].wait()
    copies[2].wait()
    ids = names[...]
    local = jnp.zeros((8, 128), jnp.float32)
    for offset in (-1, 0, 1):
        row = owner_of(offset) * FAC_DEV // 128
        values = jnp.broadcast_to(impedance[pl.ds(row, 1), :], (8, 128))
        local = jnp.where(ids // 128 == row, jnp.take_along_axis(values, ids % 128, axis=1), local)
    for z in range(depth_z):
        slot = slots[z]
        found = jnp.take_along_axis(local, jnp.maximum(slot - 1, 0), axis=1)
        damping[z] = jnp.where(slot > 0, found, 0.0)

    copies[0].wait()
    copies[1].wait()

    def load(f, s):
        z = z_of(s, depth_z)
        if f < 4:
            return adjoint[1, f, z]
        if f < 8:
            return adjoint[0, f - 4, z]
        if f < 11:
            return wind[f - 8, z]
        return damping[z]

    for i, (f, t) in enumerate(Z_PLANES):
        zb[i] = load(f, t - 1)
    even_y = lax.rem(lax.axis_index("gy"), 2) == 0
    for side in range(sides):
        send_high = even_y if side == 0 else jnp.logical_not(even_y)
        for i, row in enumerate(pack_lanes(load, own_planes(depth_z), send_high)):
            ys[side][i] = row
        for i, row in enumerate(pack_lanes(lambda f, t: load(f, t - 1), D_PLANES, send_high)):
            ds[side][i] = row
    even_x = lax.rem(lax.axis_index("gx"), 2) == 0
    rows = row_iota()
    planes = own_planes(depth_z)
    for i in range(len(planes) // 2):
        first, second = load(*planes[2 * i]), load(*planes[2 * i + 1])
        xa[i] = pack_rows(first, second, even_x, rows)
        xb[i] = pack_rows(first, second, jnp.logical_not(even_x), rows)


def edge_kernel(sides, zb, *rest):
    ys = rest[:sides]
    ds = rest[sides:2 * sides]
    xa, xb = rest[2 * sides:]
    loads = [functools.partial(lambda i: zb[i], Z_PLANES.index(p)) for p in E_PLANES]
    for ref in ys + ds:
        loads += [functools.partial(lambda ref, i: ref[i], ref, i) for i in range(ref.shape[0])]
    even_x = lax.rem(lax.axis_index("gx"), 2) == 0
    rows = row_iota()
    for i in range(len(loads) // 2):
        first, second = loads[2 * i](), loads[2 * i + 1]()
        xa[i] = pack_rows(first, second, even_x, rows)
        xb[i] = pack_rows(first, second, jnp.logical_not(even_x), rows)


def coupled(middle, c, k):
    if c == 0:
        return middle[1 + k]
    if c == 1 + k:
        return middle[0]
    return None


def flux(wind, middle, c, k):
    value = wind * middle[c]
    other = coupled(middle, c, k)
    return value if other is None else value + other


def put(cells, f, slot, tx, ty, value):
    cells[f, slot, 8 * tx:8 * tx + 8, 128 * ty:128 * ty + 128] = value


def spread(packed, j, side):
    lanes = lane_iota()
    high = (lax.rem(lax.axis_index("gy"), 2) == 0) == (side == 0)
    shift = lax.rem(256 - DEPTH * j - jnp.where(high, 0, DEPTH), 128)
    start = jnp.where(high, 0, 128 - DEPTH)
    return jnp.where((lanes >= start) & (lanes < start + DEPTH), pltpu.roll(packed, shift, 1), 0.0)


def spread_y(cells, depth_z, tx, groups):
    planes = own_planes(depth_z)
    for i, (f, s) in enumerate(planes):
        value = sum(spread(rows[i // GROUPS], i % GROUPS, side) for side, rows in enumerate(groups))
        put(cells, f, DEPTH + s, tx, 1, value)
    for i, (f, t) in enumerate(D_PLANES):
        value = sum(spread(rows[-1], i, side) for side, rows in enumerate(groups))
        put(cells, f, DEPTH - t, tx, 1, value)


def fill_kernel(sides, adjoint, wind, damping, saved_source, zb, *rest):
    ys = rest[:sides]
    ds = rest[sides:2 * sides]
    oa, ob, cells, saved, sem = rest[2 * sides:]
    copy = pltpu.make_async_copy(saved_source, saved, sem)
    copy.start()
    depth_z = damping.shape[0]
    rows = row_iota()
    even_x = lax.rem(lax.axis_index("gx"), 2) == 0
    zero = jnp.zeros((8, 128), jnp.float32)
    for s in range(depth_z):
        z = z_of(s, depth_z)
        for f in range(4):
            put(cells, f, DEPTH + s, 0, 0, adjoint[1, f, z])
            put(cells, 4 + f, DEPTH + s, 0, 0, adjoint[0, f, z])
        for f in range(3):
            put(cells, 8 + f, DEPTH + s, 0, 0, wind[f, z])
        put(cells, 11, DEPTH + s, 0, 0, damping[z])
    for i, (f, t) in enumerate(Z_PLANES):
        put(cells, f, DEPTH - t, 0, 0, zb[i])
    planes = own_planes(depth_z)
    for i in range(len(planes) // 2):
        pair = unpack_rows(oa[i], ob[i], even_x, rows)
        for (f, s), value in zip(planes[2 * i:2 * i + 2], pair):
            put(cells, f, DEPTH + s, 1, 0, value)
    spread_y(cells, depth_z, 0, [[r[i] for r in (y, d) for i in range(r.shape[0])] for y, d in zip(ys, ds)])
    for tx in range(2):
        for ty in range(2):
            for f in range(9):
                put(cells, f, DEPTH + depth_z, tx, ty, zero)
            if tx + ty:
                for f in (0, 1, 2, 3, 8):
                    put(cells, f, 0, tx, ty, zero)
                for f in (4, 5, 6, 7, 9, 10, 11):
                    if not (f == 9 and ty == 0) and not (f == 10 and ty == 1):
                        put(cells, f, 1, tx, ty, zero)
    copy.wait()


def step_kernel(sides, cells_in, ea, eb, saved, slots, table, cells, own, part_a, part_b, prod, acc):
    del cells_in
    depth_z = slots.shape[0]
    rows = row_iota()
    even_x = lax.rem(lax.axis_index("gx"), 2) == 0
    far = DEPTH + depth_z
    edges = []
    for i in range(ea.shape[0]):
        edges += unpack_rows(ea[i], eb[i], even_x, rows)
    for (f, t), value in zip(E_PLANES, edges):
        put(cells, f, DEPTH - t, 1, 0, value)
    edges = edges[len(E_PLANES):]
    y_rows = len(edges) // sides - 1
    spread_y(cells, depth_z, 1, [
        edges[side * y_rows:(side + 1) * y_rows] + [edges[sides * y_rows + side]] for side in range(sides)
    ])

    grid_row = lax.broadcasted_iota(jnp.int32, (16, 256), 0)
    grid_lane = lax.broadcasted_iota(jnp.int32, (16, 256), 1)
    x, y = lax.axis_index("gx"), lax.axis_index("gy")
    row_end = jnp.where(x == lax.axis_size("gx") - 1, 8, 12)
    row_restart = jnp.where(x == 0, 16, 12)
    lane_end = jnp.where(y == lax.axis_size("gy") - 1, 128, 192)
    lane_restart = jnp.where(y == 0, 256, 192)
    inside = (grid_row < row_end) | (grid_row >= row_restart)
    inside &= (grid_lane < lane_end) | (grid_lane >= lane_restart)
    factor = jnp.where(inside, jnp.float32(0.5 * SCALE), 0.0)
    sign = z_sign()

    def full_step(first, middle_at, upper_at):
        def body(slot, carry):
            middle = [cells[middle_at + c, slot] for c in range(4)]
            above = [cells[middle_at + c, slot + 1] for c in range(4)]
            below = [cells[middle_at + c, slot - 1] for c in range(4)]
            wind_up, wind_down = cells[8, slot + 1], cells[8, slot - 1]
            wind_x, wind_y = cells[9, slot], cells[10, slot]
            loss = SCALE * cells[11, slot]
            for c in range(4):
                total = sign * (flux(wind_up, above, c, 0) - flux(wind_down, below, c, 0))
                along = flux(wind_x, middle, c, 1)
                total += pltpu.roll(along, 15, 0) - pltpu.roll(along, 1, 0)
                along = flux(wind_y, middle, c, 2)
                total += pltpu.roll(along, 255, 1) - pltpu.roll(along, 1, 1)
                cells[upper_at + c, slot] = cells[upper_at + c, slot] + factor * total - loss * middle[c]
            return carry

        lax.fori_loop(first, far, body, 0)

    def products(step, middle_at, slot, z):
        return sum(cells[middle_at + c, slot, 0:8, 0:128] * saved[step, c, z] for c in range(4))

    full_step(1, 0, 4)
    for s in range(depth_z):
        z = z_of(s, depth_z)
        prod[z] = products(0, 0, DEPTH + s, z) + products(1, 4, DEPTH + s, z)
    full_step(2, 4, 0)
    full_step(3, 0, 4)
    for s in range(depth_z):
        z = z_of(s, depth_z)
        prod[z] = -SCALE * (prod[z] + (products(2, 0, DEPTH + s, z) + products(3, 4, DEPTH + s, z)))

    slot_count = table.shape[1]
    level = lax.broadcasted_iota(jnp.int32, (slot_count, 128), 0) + 1
    acc[...] = jnp.zeros((slot_count, 128), jnp.float32)

    def by_slot(z, carry):
        total = acc[...]
        for row in range(8):
            cell_slot = jnp.broadcast_to(slots[z, row:row + 1, :], (slot_count, 128))
            term = jnp.broadcast_to(prod[z, row:row + 1, :], (slot_count, 128))
            total = total + jnp.where(cell_slot == level, term, 0.0)
        acc[...] = total
        return carry

    lax.fori_loop(0, depth_z, by_slot, 0)
    slot_terms = jnp.sum(acc[...], axis=1, keepdims=True)
    names = jnp.broadcast_to(table[...], (slot_count, slot_count))
    diagonal = lax.broadcasted_iota(jnp.int32, (slot_count, slot_count), 0) == lax.broadcasted_iota(
        jnp.int32, (slot_count, slot_count), 1
    )
    column = jnp.sum(jnp.where(diagonal, names, 0).astype(jnp.float32), axis=1, keepdims=True)
    lane = lax.broadcasted_iota(jnp.int32, (slot_count, 128), 1)

    def bucket(offset):
        target = jnp.where(lane < FAC_DEV, owner_of(offset) * FAC_DEV + lane, -1).astype(jnp.float32)
        return jnp.sum(jnp.where(column == target, slot_terms, 0.0), axis=0, keepdims=True)

    upward, downward = bucket(1), bucket(-1)
    own[...] = bucket(0)
    part_a[...] = jnp.where(even_x, upward, downward)
    part_b[...] = jnp.where(even_x, downward, upward)


def last_kernel(cells, out):
    middle_at, upper_at = 4, 0
    depth_z = out.shape[2]
    sign = z_sign()
    def body(s, carry):
        slot = DEPTH + s
        own_part = (slice(0, 8), slice(0, 128))
        middle = [cells[(middle_at + c, slot) + own_part] for c in range(4)]
        above = [cells[(middle_at + c, slot + 1) + own_part] for c in range(4)]
        below = [cells[(middle_at + c, slot - 1) + own_part] for c in range(4)]
        mid_x = [cells[middle_at + c, slot, :, 0:128] for c in range(4)]
        mid_y = [cells[middle_at + c, slot, 0:8, :] for c in range(4)]
        wind_up, wind_down = cells[(8, slot + 1) + own_part], cells[(8, slot - 1) + own_part]
        wind_x, wind_y = cells[9, slot, :, 0:128], cells[10, slot, 0:8, :]
        loss = SCALE * cells[(11, slot) + own_part]
        z = z_of(s, depth_z)
        for c in range(4):
            total = sign * (flux(wind_up, above, c, 0) - flux(wind_down, below, c, 0))
            along = flux(wind_x, mid_x, c, 1)
            total += (pltpu.roll(along, 15, 0) - pltpu.roll(along, 1, 0))[0:8]
            along = flux(wind_y, mid_y, c, 2)
            total += (pltpu.roll(along, 255, 1) - pltpu.roll(along, 1, 1))[:, 0:128]
            upper = cells[(upper_at + c, slot) + own_part]
            out[0, c, z] = middle[c]
            out[1, c, z] = upper + jnp.float32(0.5 * SCALE) * total - loss * middle[c]
        return carry

    lax.fori_loop(0, depth_z, body, 0)


def swap_a(block, axis):
    return lax.ppermute(block, axis, [(i, i ^ 1) for i in range(lax.axis_size(axis))])


def swap_b(block, axis, wrap=False):
    count = lax.axis_size(axis)
    pairs = [(i, (i + 1 if i % 2 else i - 1) % count) for i in range(count)]
    if not wrap:
        pairs = pairs[1:-1]
    return lax.ppermute(block, axis, pairs)


def swap_diagonal(block, side):
    count_y, count_z = lax.axis_size("gy"), lax.axis_size("gz")
    pairs = []
    for y in range(count_y):
        step = 1 if (y % 2 == 0) == (side == 0) else -1
        if 0 <= y + step < count_y:
            pairs += [(y * count_z + z, (y + step) * count_z + (z ^ 1)) for z in range(count_z)]
    return lax.ppermute(block, ("gy", "gz"), pairs)


VMEM = pl.BlockSpec(memory_space=pltpu.VMEM)
HBM = pl.BlockSpec(memory_space=pltpu.HBM)


def call(kernel, name, limit, in_specs, out_shape, scratch=(), aliases=None, cost=None):
    return pl.pallas_call(
        kernel,
        out_shape=[jax.ShapeDtypeStruct(o.shape, o.dtype) for o in out_shape],
        in_specs=in_specs,
        out_specs=[VMEM] * len(out_shape),
        scratch_shapes=list(scratch),
        input_output_aliases=aliases or {},
        compiler_params=pltpu.CompilerParams(vmem_limit_bytes=limit << 20),
        cost_estimate=cost and pl.CostEstimate(flops=cost, bytes_accessed=cost, transcendentals=0),
        name=name,
    )


def in_hbm(array):
    return pltpu.with_memory_space_constraint(array, pltpu.HBM)


def rows_of(count):
    return jax.ShapeDtypeStruct((count, 8, 128), jnp.float32)


def local(adjoint, saved_state, wind_field, facade_slot, facade_table, impedance):
    depth_z = facade_slot.shape[0]
    sides = 1 if lax.axis_size("gy") == 2 else 2
    table = facade_table.reshape(1, -1)
    rates = impedance.reshape(-1, 128)
    own_count = FIELDS * depth_z
    y_rows = -(-own_count // GROUPS)
    packed = call(
        functools.partial(pack_kernel, sides),
        "pack", 4,
        [HBM] * 5,
        [adjoint, wind_field, facade_slot, table, rows_of(depth_z), rows_of(len(Z_PLANES))]
        + [rows_of(y_rows)] * sides
        + [rows_of(1)] * sides
        + [rows_of(own_count // 2)] * 2,
        [pltpu.VMEM(rates.shape, jnp.float32), pltpu.VMEM((8, 128), jnp.int32), pltpu.SemaphoreType.DMA((5,))],
    )(*map(in_hbm, (adjoint, wind_field, facade_slot, table, rates)))
    adjoint, wind, slots, table, damping, zb = packed[:6]
    ys, ds = packed[6:6 + sides], packed[6 + sides:6 + 2 * sides]
    xa, xb = packed[6 + 2 * sides:]
    with jax.named_scope("z_swap"):
        zb = swap_a(zb, "gz")
    with jax.named_scope("y_swap"):
        ys = [swap_a(b, "gy") if side == 0 else swap_b(b, "gy") for side, b in enumerate(ys)]
    with jax.named_scope("d_swap"):
        ds = [swap_diagonal(b, side) for side, b in enumerate(ds)]
    with jax.named_scope("x_swap"):
        xb = swap_b(xb, "gx")
        xa = swap_a(xa, "gx")
    edge_count = (len(E_PLANES) + sides * (y_rows + 1)) // 2
    ea, eb = call(
        functools.partial(edge_kernel, sides),
        "edges", 2,
        [VMEM] * (1 + 2 * sides),
        [rows_of(edge_count)] * 2,
    )(zb, *ys, *ds)
    with jax.named_scope("e_swap"):
        eb = swap_b(eb, "gx")
        ea = swap_a(ea, "gx")
    cells = jax.ShapeDtypeStruct((FIELDS, DEPTH + depth_z + 1, 16, 256), jnp.float32)
    cells, saved = call(
        functools.partial(fill_kernel, sides),
        "fill", 2,
        [VMEM] * 3 + [HBM] + [VMEM] * (3 + 2 * sides),
        [cells, saved_state],
        [pltpu.SemaphoreType.DMA],
        cost=4000000,
    )(adjoint, wind, damping, in_hbm(saved_state), zb, *ys, *ds, xa, xb)
    row = jax.ShapeDtypeStruct((1, 128), jnp.float32)
    cells, own, part_a, part_b = call(
        functools.partial(step_kernel, sides),
        "steps", 2,
        [VMEM] * 6,
        [cells, row, row, row],
        [pltpu.VMEM((depth_z, 8, 128), jnp.float32), pltpu.VMEM((table.shape[1], 128), jnp.float32)],
        aliases={0: 0},
    )(cells, ea, eb, saved, slots, table)
    with jax.named_scope("g_swap"):
        part_b = swap_b(part_b, "gx", wrap=True)
        part_a = swap_a(part_a, "gx")
    out, = call(last_kernel, "last", 2, [VMEM], [adjoint], cost=4000000)(cells)
    gradient = (own + part_a + part_b)[0, :FAC_DEV]
    return out, gradient


def solution(mesh):
    return jax.shard_map(
        local,
        mesh=mesh,
        in_specs=(
            P(None, None, "gz", "gx", "gy"),
            P(None, None, "gz", "gx", "gy"),
            P(None, "gz", "gx", "gy"),
            P("gz", "gx", "gy"),
            P("gz", "gx", "gy", None),
            P(),
        ),
        out_specs=(P(None, None, "gz", "gx", "gy"), P(("gx", "gy", "gz"))),
        check_vma=False,
    )
```

```python
import functools

import jax
import jax.numpy as jnp
import numpy as np
from jax import lax
from jax.experimental import pallas as pl
from jax.experimental.pallas import tpu as pltpu
from jax.sharding import PartitionSpec as P


FAC_DEV = 32
TIME_STEP = 0.3
SCALE = 2.0 * TIME_STEP

FIELDS = 12
DEPTH = 4
GROUP = 2 * DEPTH
E_PLANES = [(f, t) for t in (1, 2) for f in range(FIELDS)] + [(f, 3) for f in (0, 1, 2, 3, 8, 9)]
R_PLANES = [(f, 3) for f in (4, 5, 6, 7, 10, 11)] + [(f, 4) for f in (0, 1, 2, 3, 8)]
Y_ROWS = FIELDS // 2
D_ROWS = FIELDS // 4


def z_of(s, depth_z):
    return jnp.where(lax.axis_index("gz") == 0, depth_z - 1 - s, s)


def z_sign():
    return jnp.where(lax.axis_index("gz") == 0, jnp.float32(-1.0), jnp.float32(1.0))


def own_planes(depth_z):
    return [(f, s) for f in range(FIELDS) for s in range(depth_z)]


def iota(dim, shape=(8, 128)):
    return lax.broadcasted_iota(jnp.int32, shape, dim)


def is_even(axis):
    return lax.rem(lax.axis_index(axis), 2) == 0


def at_end(axis):
    return (lax.axis_index(axis) == 0) | (lax.axis_index(axis) == lax.axis_size(axis) - 1)


def pack_groups(planes, load):
    groups = iota(1) // GROUP
    row = jnp.zeros((8, 128), jnp.float32)
    for group, plane in planes:
        edge = pltpu.roll(load(*plane), (GROUP * group + DEPTH) % 128, 1)
        row = jnp.where(groups == group, edge, row)
    return row


def unpack_strip(f, y_rows, d_rows):
    lanes = iota(1)
    start = DEPTH * GROUP
    own = pltpu.roll(y_rows[f // 2], (start - 64 * (f % 2)) % 128, 1)
    beyond = y_shift(d_rows[f // 4], -32 * (f % 4))
    return jnp.where(lanes < start, beyond, jnp.where(lanes < start + 64, own, 0.0))


def y_shift(row, shift):
    return pltpu.roll(row, shift % 128, 1) if shift % 128 else row


def merge_sides(parts):
    k = iota(1) % GROUP
    even = is_even("gy")
    if len(parts) == 1:
        start = jnp.where(even, DEPTH, 0)
        return jnp.where((k >= start) & (k < start + DEPTH), parts[0], 0.0)
    second = jnp.where(at_end("gy"), 0.0, parts[1])
    return jnp.where(k >= DEPTH, jnp.where(even, parts[0], second), jnp.where(even, second, parts[0]))


def merged_rows(refs):
    return [merge_sides([ref[i] for ref in refs]) for i in range(refs[0].shape[0])]


def pack_rows(first, second, send_high, rows):
    turned = pltpu.roll(second, 4, 0)
    low = jnp.where(rows < 4, first, turned)
    high = jnp.where(rows < 4, turned, first)
    return jnp.where(send_high, high, low)


def unpack_rows(got_a, got_b, even, rows):
    got_b = jnp.where(at_end("gx"), 0.0, got_b)
    from_high = jnp.where(even, got_a, got_b)
    from_low = jnp.where(even, got_b, got_a)
    first = jnp.where(rows < 4, from_high, from_low)
    second = pltpu.roll(jnp.where(rows < 4, from_low, from_high), 4, 0)
    return first, second


def pack_pairs(planes, xa, xb):
    even = is_even("gx")
    rows = iota(0)
    for i in range(-(-len(planes) // 2)):
        first = planes[2 * i]()
        second = planes[2 * i + 1]() if 2 * i + 1 < len(planes) else first
        xa[i] = pack_rows(first, second, even, rows)
        xb[i] = pack_rows(first, second, jnp.logical_not(even), rows)


def unpack_pairs(xa, xb):
    even = is_even("gx")
    rows = iota(0)
    values = []
    for i in range(xa.shape[0]):
        values += unpack_rows(xa[i], xb[i], even, rows)
    return values


def owner_of(offset):
    count_x, count_y, count_z = (lax.axis_size(a) for a in ("gx", "gy", "gz"))
    x = lax.rem(lax.axis_index("gx") + (offset + count_x), count_x)
    return (x * count_y + lax.axis_index("gy")) * count_z + lax.axis_index("gz")


def loader(adjoint, wind, damping):
    depth_z = damping.shape[0]

    def load(f, s):
        z = z_of(s, depth_z)
        if f < 4:
            return adjoint[1, f, z]
        if f < 8:
            return adjoint[0, f - 4, z]
        if f < 11:
            return wind[f - 8, z]
        return damping[z]

    return load


def pack_kernel(*refs):
    sources = refs[:5]
    adjoint, wind, slots, table, damping, zb, yb, db, impedance, names, sems = refs[5:]
    targets = (adjoint, wind, slots, table, impedance)
    copies = [pltpu.make_async_copy(a, b, sems.at[i]) for i, (a, b) in enumerate(zip(sources, targets))]
    for i in (3, 4, 2, 0, 1):
        copies[i].start()
    depth_z = slots.shape[0]
    names[...] = jnp.zeros((8, 128), jnp.int32)
    copies[3].wait()
    names[:, :table.shape[1]] = jnp.broadcast_to(table[...], (8, table.shape[1]))
    copies[4].wait()
    copies[2].wait()
    ids = names[...]
    local = jnp.zeros((8, 128), jnp.float32)
    for offset in (-1, 0, 1):
        row = owner_of(offset) * FAC_DEV // 128
        values = jnp.broadcast_to(impedance[pl.ds(row, 1), :], (8, 128))
        local = jnp.where(ids // 128 == row, jnp.take_along_axis(values, ids % 128, axis=1), local)
    for z in range(depth_z):
        slot = slots[z]
        found = jnp.take_along_axis(local, jnp.maximum(slot - 1, 0), axis=1)
        damping[z] = jnp.where(slot > 0, found, 0.0)
    copies[0].wait()
    copies[1].wait()
    load = loader(adjoint, wind, damping)
    for i, (f, t) in enumerate(E_PLANES):
        zb[i] = load(f, t - 1)
    for i in range(Y_ROWS):
        yb[i] = pack_groups([(8 * j + s, (2 * i + j, s)) for j in range(2) for s in range(depth_z)], load)
    for i in range(D_ROWS):
        db[i] = pack_groups([(4 * j + DEPTH - t, (4 * i + j, t - 1)) for j in range(4) for t in (1, 2, 3)], load)


def pack_x_kernel(adjoint, wind, damping, zr, xa, xb):
    load = loader(adjoint, wind, damping)
    for i, (f, t) in enumerate(R_PLANES):
        zr[i] = load(f, t - 1)
    pack_pairs([functools.partial(load, *p) for p in own_planes(damping.shape[0])], xa, xb)


def edge_kernel(sides, zb, *rest):
    y_rows = merged_rows(rest[:sides])
    d_rows = merged_rows(rest[sides:2 * sides])
    planes = [functools.partial(lambda i: zb[i], i) for i in range(len(E_PLANES))]
    planes += [functools.partial(lambda row: row, row) for row in y_rows + d_rows]
    pack_pairs(planes, *rest[2 * sides:])


def coupled(middle, c, k):
    if c == 0:
        return middle[1 + k]
    if c == 1 + k:
        return middle[0]
    return None


def flux(wind, middle, c, k):
    value = wind * middle[c]
    other = coupled(middle, c, k)
    return value if other is None else value + other


def put(cells, f, slot, tx, value):
    cells[f, slot, 8 * tx:8 * tx + 8, :] = value


def fill_kernel(sides, adjoint, wind, damping, saved_source, zb, zr, *rest):
    y_rows = merged_rows(rest[:sides])
    d_rows = merged_rows(rest[sides:2 * sides])
    xa, xb, cells, strips, saved, sem = rest[2 * sides:]
    copy = pltpu.make_async_copy(saved_source, saved, sem)
    copy.start()
    depth_z = damping.shape[0]
    zero = jnp.zeros((8, 128), jnp.float32)
    load = loader(adjoint, wind, damping)
    planes = own_planes(depth_z)
    for (f, s), value in zip(planes, unpack_pairs(xa, xb)):
        put(cells, f, DEPTH + s, 0, load(f, s))
        put(cells, f, DEPTH + s, 1, value)
    for ref, places in ((zb, E_PLANES), (zr, R_PLANES)):
        for i, (f, t) in enumerate(places):
            put(cells, f, DEPTH - t, 0, ref[i])
    for f in range(FIELDS):
        strips[f, 0:8, :] = unpack_strip(f, y_rows, d_rows)
    for f in range(9):
        put(cells, f, DEPTH + depth_z, 0, zero)
        put(cells, f, DEPTH + depth_z, 1, zero)
    for f, t in R_PLANES:
        put(cells, f, DEPTH - t, 1, zero)
    copy.wait()


def y_change(main, near, lanes):
    up = pltpu.roll(jnp.where(lanes == 0, near, main), 127, 1)
    return up - pltpu.roll(jnp.where(lanes == 127, near, main), 1, 1)


def step_kernel(cells_in, strips_in, ea, eb, saved, slots, table, cells, strips, own, part_a, part_b, prod, acc):
    del cells_in, strips_in
    depth_z = slots.shape[0]
    far = DEPTH + depth_z
    edges = unpack_pairs(ea, eb)
    for (f, t), value in zip(E_PLANES, edges):
        put(cells, f, DEPTH - t, 1, value)
    start = len(E_PLANES)
    for f in range(FIELDS):
        strips[f, 8:16, :] = unpack_strip(f, edges[start:start + Y_ROWS], edges[start + Y_ROWS:])

    tile = (16, 128)
    rows, lanes = iota(0, tile), iota(1, tile)
    groups, k = lanes // GROUP, lanes % GROUP
    x, y = lax.axis_index("gx"), lax.axis_index("gy")
    row_end = jnp.where(x == lax.axis_size("gx") - 1, 8, 12)
    row_restart = jnp.where(x == 0, 16, 12)
    inside = (rows < row_end) | (rows >= row_restart)
    k_first = jnp.where(y == 0, DEPTH, 0)
    k_end = jnp.where(y == lax.axis_size("gy") - 1, DEPTH, GROUP)
    factor = jnp.where(inside, jnp.float32(0.5 * SCALE), 0.0)
    side_factor = jnp.where((k >= k_first) & (k < k_end) & (lanes < GROUP * far), factor, 0.0)
    sign = z_sign()

    def full_step(first, middle_at, upper_at):
        side = [strips[middle_at + c] for c in range(4)]
        side_y = [flux(strips[10], side, c, 2) for c in range(4)]

        def body(slot, joined):
            middle = [cells[middle_at + c, slot] for c in range(4)]
            above = [cells[middle_at + c, slot + 1] for c in range(4)]
            below = [cells[middle_at + c, slot - 1] for c in range(4)]
            wind_up, wind_down = cells[8, slot + 1], cells[8, slot - 1]
            wind_x, wind_y = cells[9, slot], cells[10, slot]
            loss = SCALE * cells[11, slot]
            seen = []
            for c in range(4):
                total = sign * (flux(wind_up, above, c, 0) - flux(wind_down, below, c, 0))
                along = flux(wind_x, middle, c, 1)
                total += pltpu.roll(along, 15, 0) - pltpu.roll(along, 1, 0)
                along = flux(wind_y, middle, c, 2)
                total += y_change(along, pltpu.roll(side_y[c], 124 - GROUP * slot, 1), lanes)
                seen.append(jnp.where(groups == slot, pltpu.roll(along, GROUP * slot + DEPTH, 1), joined[c]))
                cells[upper_at + c, slot] = cells[upper_at + c, slot] + factor * total - loss * middle[c]
            return tuple(seen)

        joined = lax.fori_loop(first, far, body, tuple(jnp.zeros(tile, jnp.float32) for _ in range(4)))
        loss = SCALE * strips[11]
        for c in range(4):
            along = flux(strips[8], side, c, 0)
            total = sign * (pltpu.roll(along, 128 - GROUP, 1) - pltpu.roll(along, GROUP, 1))
            along = flux(strips[9], side, c, 1)
            total += pltpu.roll(along, 15, 0) - pltpu.roll(along, 1, 0)
            total += pltpu.roll(jnp.where(k == DEPTH, joined[c], side_y[c]), 127, 1)
            total -= pltpu.roll(jnp.where(k == DEPTH - 1, joined[c], side_y[c]), 1, 1)
            strips[upper_at + c] = strips[upper_at + c] + side_factor * total - loss * side[c]

    def products(step, middle_at, slot, z):
        return sum(cells[middle_at + c, slot, 0:8, :] * saved[step, c, z] for c in range(4))

    full_step(1, 0, 4)
    for s in range(depth_z):
        z = z_of(s, depth_z)
        prod[z] = products(0, 0, DEPTH + s, z) + products(1, 4, DEPTH + s, z)
    full_step(2, 4, 0)
    full_step(3, 0, 4)
    for s in range(depth_z):
        z = z_of(s, depth_z)
        prod[z] = -SCALE * (prod[z] + (products(2, 0, DEPTH + s, z) + products(3, 4, DEPTH + s, z)))

    slot_count = table.shape[1]
    level = iota(0, (slot_count, 128)) + 1
    acc[...] = jnp.zeros((slot_count, 128), jnp.float32)

    def by_slot(z, carry):
        total = acc[...]
        for row in range(8):
            cell_slot = jnp.broadcast_to(slots[z, row:row + 1, :], (slot_count, 128))
            term = jnp.broadcast_to(prod[z, row:row + 1, :], (slot_count, 128))
            total = total + jnp.where(cell_slot == level, term, 0.0)
        acc[...] = total
        return carry

    lax.fori_loop(0, depth_z, by_slot, 0)
    slot_terms = jnp.sum(acc[...], axis=1, keepdims=True)
    names = jnp.broadcast_to(table[...], (slot_count, slot_count))
    diagonal = iota(0, (slot_count, slot_count)) == iota(1, (slot_count, slot_count))
    column = jnp.sum(jnp.where(diagonal, names, 0).astype(jnp.float32), axis=1, keepdims=True)
    lane = iota(1, (slot_count, 128))

    def bucket(offset):
        target = jnp.where(lane < FAC_DEV, owner_of(offset) * FAC_DEV + lane, -1).astype(jnp.float32)
        return jnp.sum(jnp.where(column == target, slot_terms, 0.0), axis=0, keepdims=True)

    upward, downward = bucket(1), bucket(-1)
    own[...] = bucket(0)
    even = is_even("gx")
    part_a[...] = jnp.where(even, upward, downward)
    part_b[...] = jnp.where(even, downward, upward)


def last_kernel(cells, strips, out):
    middle_at, upper_at = 4, 0
    depth_z = out.shape[2]
    sign = z_sign()
    lanes = iota(1)
    side = [strips[middle_at + c, 0:8] for c in range(4)]
    side_y = [flux(strips[10, 0:8], side, c, 2) for c in range(4)]

    def body(s, carry):
        slot = DEPTH + s

        def plane(f, at):
            return cells[f, at, 0:8, :]

        middle = [plane(middle_at + c, slot) for c in range(4)]
        above = [plane(middle_at + c, slot + 1) for c in range(4)]
        below = [plane(middle_at + c, slot - 1) for c in range(4)]
        wide = [cells[middle_at + c, slot] for c in range(4)]
        wind_up, wind_down = plane(8, slot + 1), plane(8, slot - 1)
        wind_x, wind_y = cells[9, slot], plane(10, slot)
        loss = SCALE * plane(11, slot)
        z = z_of(s, depth_z)
        for c in range(4):
            total = sign * (flux(wind_up, above, c, 0) - flux(wind_down, below, c, 0))
            along = flux(wind_x, wide, c, 1)
            total += (pltpu.roll(along, 15, 0) - pltpu.roll(along, 1, 0))[0:8]
            along = flux(wind_y, middle, c, 2)
            total += y_change(along, pltpu.roll(side_y[c], 124 - GROUP * slot, 1), lanes)
            out[0, c, z] = middle[c]
            out[1, c, z] = plane(upper_at + c, slot) + jnp.float32(0.5 * SCALE) * total - loss * middle[c]
        return carry

    lax.fori_loop(0, depth_z, body, 0)


AXES = ("gx", "gy", "gz")


def swap(block, partner):
    counts = tuple(lax.axis_size(axis) for axis in AXES)
    pairs = []
    for place in np.ndindex(*counts):
        other = partner(*place, counts)
        pairs.append((int(np.ravel_multi_index(place, counts)), int(np.ravel_multi_index(other, counts))))
    return lax.ppermute(block, AXES, pairs)


def swap_z(x, y, z, counts):
    return x, y, z ^ 1


def swap_xa(x, y, z, counts):
    return x ^ 1, y, z


def swap_xb(x, y, z, counts):
    other = x + 1 if x % 2 else x - 1
    return (other, y, z) if 0 <= other < counts[0] else (x, y ^ 1, z)


def swap_ring(x, y, z, counts):
    return (x + 1 if x % 2 else x - 1) % counts[0], y, z


def swap_y(side, diagonal):
    def partner(x, y, z, counts):
        other = y ^ 1 if side == 0 else y + 1 if y % 2 else y - 1
        if 0 <= other < counts[1]:
            return x, other, z ^ 1 if diagonal else z
        return x, y, z ^ 1

    return partner


VMEM = pl.BlockSpec(memory_space=pltpu.VMEM)
HBM = pl.BlockSpec(memory_space=pltpu.HBM)


def call(kernel, limit, in_specs, out_shape, scratch=(), aliases=None, cost=None):
    return pl.pallas_call(
        kernel,
        out_shape=[jax.ShapeDtypeStruct(o.shape, o.dtype) for o in out_shape],
        in_specs=in_specs,
        out_specs=[VMEM] * len(out_shape),
        scratch_shapes=list(scratch),
        input_output_aliases=aliases or {},
        compiler_params=pltpu.CompilerParams(vmem_limit_bytes=limit << 20),
        cost_estimate=cost and pl.CostEstimate(flops=cost, bytes_accessed=cost, transcendentals=0),
    )


def in_hbm(array):
    return pltpu.with_memory_space_constraint(array, pltpu.HBM)


def rows_of(count):
    return jax.ShapeDtypeStruct((count, 8, 128), jnp.float32)


def local(adjoint, saved_state, wind_field, facade_slot, facade_table, impedance):
    depth_z = facade_slot.shape[0]
    sides = 1 if lax.axis_size("gy") == 2 else 2
    table = facade_table.reshape(1, -1)
    rates = impedance.reshape(-1, 128)
    adjoint, wind, slots, table, damping, zb, yb, db = call(
        pack_kernel,
        4,
        [HBM] * 5,
        [adjoint, wind_field, facade_slot, table, rows_of(depth_z), rows_of(len(E_PLANES)), rows_of(Y_ROWS), rows_of(D_ROWS)],
        [pltpu.VMEM(rates.shape, jnp.float32), pltpu.VMEM((8, 128), jnp.int32), pltpu.SemaphoreType.DMA((5,))],
    )(*map(in_hbm, (adjoint, wind_field, facade_slot, table, rates)))
    zr, xa, xb = call(
        pack_x_kernel, 2, [VMEM] * 3, [rows_of(len(R_PLANES))] + [rows_of(FIELDS * depth_z // 2)] * 2, cost=400000
    )(adjoint, wind, damping)
    zb = swap(zb, swap_z)
    ds = [swap(db, swap_y(side, True)) for side in range(sides)]
    ys = [swap(yb, swap_y(side, False)) for side in range(sides)]
    xa = swap(xa, swap_xa)
    xb = swap(xb, swap_xb)
    zr = swap(zr, swap_z)
    edge_count = (len(E_PLANES) + Y_ROWS + D_ROWS + 1) // 2
    ea, eb = call(
        functools.partial(edge_kernel, sides), 2, [VMEM] * (1 + 2 * sides), [rows_of(edge_count)] * 2
    )(zb, *ys, *ds)
    ea = swap(ea, swap_xa)
    eb = swap(eb, swap_xb)
    cells = jax.ShapeDtypeStruct((FIELDS, DEPTH + depth_z + 1, 16, 128), jnp.float32)
    strips = jax.ShapeDtypeStruct((FIELDS, 16, 128), jnp.float32)
    cells, strips, saved = call(
        functools.partial(fill_kernel, sides),
        2,
        [VMEM] * 3 + [HBM] + [VMEM] * (4 + 2 * sides),
        [cells, strips, saved_state],
        [pltpu.SemaphoreType.DMA],
        cost=4000000,
    )(adjoint, wind, damping, in_hbm(saved_state), zb, zr, *ys, *ds, xa, xb)
    row = jax.ShapeDtypeStruct((1, 128), jnp.float32)
    cells, strips, own, part_a, part_b = call(
        step_kernel,
        2,
        [VMEM] * 7,
        [cells, strips, row, row, row],
        [pltpu.VMEM((depth_z, 8, 128), jnp.float32), pltpu.VMEM((table.shape[1], 128), jnp.float32)],
        aliases={0: 0, 1: 1},
    )(cells, strips, ea, eb, saved, slots, table)
    part_b = swap(part_b, swap_ring)
    part_a = swap(part_a, swap_xa)
    out, = call(last_kernel, 2, [VMEM] * 2, [adjoint], cost=4000000)(cells, strips)
    gradient = (own + part_a + part_b)[0, :FAC_DEV]
    return out, gradient


def solution(mesh):
    return jax.shard_map(
        local,
        mesh=mesh,
        in_specs=(
            P(None, None, "gz", "gx", "gy"),
            P(None, None, "gz", "gx", "gy"),
            P(None, "gz", "gx", "gy"),
            P("gz", "gx", "gy"),
            P("gz", "gx", "gy", None),
            P(),
        ),
        out_specs=(P(None, None, "gz", "gx", "gy"), P(("gx", "gy", "gz"))),
        check_vma=False,
    )
```

```python
import functools

import jax
import jax.numpy as jnp
import numpy as np
from jax import lax
from jax.experimental import pallas as pl
from jax.experimental.pallas import tpu as pltpu
from jax.sharding import PartitionSpec as P


FAC_DEV = 32
TIME_STEP = 0.3
SCALE = 2.0 * TIME_STEP

FIELDS = 12
DEPTH = 4
BASE = DEPTH + 1
GROUP = 2 * DEPTH
CHUNK = 6
E_PLANES = [(f, t) for t in (1, 2) for f in range(FIELDS)] + [(f, 3) for f in (0, 1, 2, 3, 8, 9)]
R_PLANES = [(f, 3) for f in (4, 5, 6, 7, 10, 11)] + [(f, 4) for f in (0, 1, 2, 3, 8)]
Y_ROWS = FIELDS // 2
D_ROWS = FIELDS // 4


def z_of(s, depth_z):
    return jnp.where(lax.axis_index("gz") == 0, depth_z - 1 - s, s)


def z_sign():
    return jnp.where(lax.axis_index("gz") == 0, jnp.float32(-1.0), jnp.float32(1.0))


def own_planes(depth_z):
    return [(f, s) for f in range(FIELDS) for s in range(depth_z)]


def iota(dim, shape=(8, 128)):
    return lax.broadcasted_iota(jnp.int32, shape, dim)


def is_even(axis):
    return lax.rem(lax.axis_index(axis), 2) == 0


def at_end(axis):
    return (lax.axis_index(axis) == 0) | (lax.axis_index(axis) == lax.axis_size(axis) - 1)


def pack_groups(planes, load):
    groups = iota(1) // GROUP
    row = jnp.zeros((8, 128), jnp.float32)
    for group, plane in planes:
        edge = pltpu.roll(load(*plane), (GROUP * group + DEPTH) % 128, 1)
        row = jnp.where(groups == group, edge, row)
    return row


def unpack_strip(f, y_rows, d_rows):
    lanes = iota(1)
    start = BASE * GROUP
    own = pltpu.roll(y_rows[f // 2], (start - 64 * (f % 2)) % 128, 1)
    beyond = y_shift(d_rows[f // 4], GROUP - 32 * (f % 4))
    return jnp.where(lanes < start, beyond, jnp.where(lanes < start + 64, own, 0.0))


def y_shift(row, shift):
    return pltpu.roll(row, shift % 128, 1) if shift % 128 else row


def merge_sides(parts):
    k = iota(1) % GROUP
    even = is_even("gy")
    if len(parts) == 1:
        start = jnp.where(even, DEPTH, 0)
        return jnp.where((k >= start) & (k < start + DEPTH), parts[0], 0.0)
    second = jnp.where(at_end("gy"), 0.0, parts[1])
    return jnp.where(k >= DEPTH, jnp.where(even, parts[0], second), jnp.where(even, second, parts[0]))


def merged_rows(refs):
    return [merge_sides([ref[i] for ref in refs]) for i in range(refs[0].shape[0])]


def pack_rows(first, second, send_high, rows):
    turned = pltpu.roll(second, 4, 0)
    low = jnp.where(rows < 4, first, turned)
    high = jnp.where(rows < 4, turned, first)
    return jnp.where(send_high, high, low)


def unpack_rows(got_a, got_b, even, rows):
    got_b = jnp.where(at_end("gx"), 0.0, got_b)
    from_high = jnp.where(even, got_a, got_b)
    from_low = jnp.where(even, got_b, got_a)
    first = jnp.where(rows < 4, from_high, from_low)
    second = pltpu.roll(jnp.where(rows < 4, from_low, from_high), 4, 0)
    return first, second


def pack_pairs(planes, xa, xb):
    even = is_even("gx")
    rows = iota(0)
    for i in range(-(-len(planes) // 2)):
        first = planes[2 * i]()
        second = planes[2 * i + 1]() if 2 * i + 1 < len(planes) else first
        xa[i] = pack_rows(first, second, even, rows)
        xb[i] = pack_rows(first, second, jnp.logical_not(even), rows)


def unpack_pairs(xa, xb):
    even = is_even("gx")
    rows = iota(0)
    values = []
    for i in range(xa.shape[0]):
        values += unpack_rows(xa[i], xb[i], even, rows)
    return values


def owner_of(offset):
    count_x, count_y, count_z = (lax.axis_size(a) for a in ("gx", "gy", "gz"))
    x = lax.rem(lax.axis_index("gx") + (offset + count_x), count_x)
    return (x * count_y + lax.axis_index("gy")) * count_z + lax.axis_index("gz")


def loader(adjoint, wind, damping):
    depth_z = damping.shape[0]

    def load(f, s):
        z = z_of(s, depth_z)
        if f < 4:
            return adjoint[1, f, z]
        if f < 8:
            return adjoint[0, f - 4, z]
        if f < 11:
            return wind[f - 8, z]
        return damping[z]

    return load


def pack_kernel(*refs):
    sources = refs[:5]
    adjoint, wind, slots, table, damping, zb, yb, db, impedance, names, sems = refs[5:]
    targets = (adjoint, wind, slots, table, impedance)
    copies = [pltpu.make_async_copy(a, b, sems.at[i]) for i, (a, b) in enumerate(zip(sources, targets))]
    for i in (3, 4, 2, 0, 1):
        copies[i].start()
    depth_z = slots.shape[0]
    names[...] = jnp.zeros((8, 128), jnp.int32)
    copies[3].wait()
    names[:, :table.shape[1]] = jnp.broadcast_to(table[...], (8, table.shape[1]))
    copies[4].wait()
    copies[2].wait()
    ids = names[...]
    local = jnp.zeros((8, 128), jnp.float32)
    for offset in (-1, 0, 1):
        row = owner_of(offset) * FAC_DEV // 128
        values = jnp.broadcast_to(impedance[pl.ds(row, 1), :], (8, 128))
        local = jnp.where(ids // 128 == row, jnp.take_along_axis(values, ids % 128, axis=1), local)
    for z in range(depth_z):
        slot = slots[z]
        found = jnp.take_along_axis(local, jnp.maximum(slot - 1, 0), axis=1)
        damping[z] = jnp.where(slot > 0, found, 0.0)
    copies[0].wait()
    copies[1].wait()
    load = loader(adjoint, wind, damping)
    for i, (f, t) in enumerate(E_PLANES + R_PLANES):
        zb[i] = load(f, t - 1)
    for i in range(Y_ROWS):
        yb[i] = pack_groups([(8 * j + s, (2 * i + j, s)) for j in range(2) for s in range(depth_z)], load)
    for i in range(D_ROWS):
        db[i] = pack_groups([(4 * j + DEPTH - t, (4 * i + j, t - 1)) for j in range(4) for t in (1, 2, 3)], load)


def pack_x_kernel(adjoint, wind, damping, xa, xb):
    load = loader(adjoint, wind, damping)
    pack_pairs([functools.partial(load, *p) for p in own_planes(damping.shape[0])], xa, xb)


def edge_kernel(sides, zb, *rest):
    y_rows = merged_rows(rest[:sides])
    d_rows = merged_rows(rest[sides:2 * sides])
    planes = [functools.partial(lambda i: zb[i], i) for i in range(len(E_PLANES))]
    planes += [functools.partial(lambda row: row, row) for row in y_rows + d_rows]
    pack_pairs(planes, *rest[2 * sides:])


def coupled(middle, c, k):
    if c == 0:
        return middle[1 + k]
    if c == 1 + k:
        return middle[0]
    return None


def flux(wind, middle, c, k):
    value = wind * middle[c]
    other = coupled(middle, c, k)
    return value if other is None else value + other


def put(cells, f, slot, tx, value):
    cells[f, slot, 8 * tx:8 * tx + 8, :] = value


def fetch_kernel(source, target, sem):
    copy = pltpu.make_async_copy(source, target, sem)
    copy.start()
    copy.wait()


def fill_kernel(sides, adjoint, wind, damping, zb, *rest):
    y_rows = merged_rows(rest[:sides])
    d_rows = merged_rows(rest[sides:2 * sides])
    xa, xb, cells, strips = rest[2 * sides:]
    depth_z = damping.shape[0]
    zero = jnp.zeros((8, 128), jnp.float32)
    load = loader(adjoint, wind, damping)
    planes = own_planes(depth_z)
    for (f, s), value in zip(planes, unpack_pairs(xa, xb)):
        put(cells, f, BASE + s, 0, load(f, s))
        put(cells, f, BASE + s, 1, value)
    for i, (f, t) in enumerate(E_PLANES + R_PLANES):
        put(cells, f, BASE - t, 0, zb[i])
    for f in range(FIELDS):
        strips[f, 0:8, :] = unpack_strip(f, y_rows, d_rows)
    for tx in range(2):
        for f in range(9):
            put(cells, f, BASE + depth_z, tx, zero)
        for f in (0, 1, 2, 3, 8):
            put(cells, f, 0, tx, zero)
        for f in (4, 5, 6, 7, 9, 10, 11):
            put(cells, f, 1, tx, zero)
    for f, t in R_PLANES:
        put(cells, f, BASE - t, 1, zero)


def y_change(main, side, slot, lanes):
    above = pltpu.roll(side, 127 - DEPTH - GROUP * slot, 1)
    below = pltpu.roll(side, 129 - DEPTH - GROUP * slot, 1)
    up = jnp.where(lanes == 127, above, pltpu.roll(main, 127, 1))
    return up - jnp.where(lanes == 0, below, pltpu.roll(main, 1, 1))


def step_kernel(cells_in, strips_in, ea, eb, saved, slots, table, cells, strips, own, part_a, part_b, prod, acc):
    del cells_in, strips_in
    depth_z = slots.shape[0]
    far = BASE + depth_z
    edges = unpack_pairs(ea, eb)
    for (f, t), value in zip(E_PLANES, edges):
        put(cells, f, BASE - t, 1, value)
    start = len(E_PLANES)
    for f in range(FIELDS):
        strips[f, 8:16, :] = unpack_strip(f, edges[start:start + Y_ROWS], edges[start + Y_ROWS:])

    tile = (16, 128)
    rows, lanes = iota(0, tile), iota(1, tile)
    groups, k = lanes // GROUP, lanes % GROUP
    x, y = lax.axis_index("gx"), lax.axis_index("gy")
    row_end = jnp.where(x == lax.axis_size("gx") - 1, 8, 12)
    row_restart = jnp.where(x == 0, 16, 12)
    inside = (rows < row_end) | (rows >= row_restart)
    k_first = jnp.where(y == 0, DEPTH, 0)
    k_end = jnp.where(y == lax.axis_size("gy") - 1, DEPTH, GROUP)
    factor = jnp.where(inside, jnp.float32(0.5 * SCALE), 0.0)
    side_factor = jnp.where((k >= k_first) & (k < k_end) & (lanes < GROUP * far), factor, 0.0)
    sign = z_sign()

    def full_step(halo, middle_at, upper_at):
        first = far - -(-(depth_z + halo) // CHUNK) * CHUNK
        side = [strips[middle_at + c] for c in range(4)]
        side_y = [flux(strips[10], side, c, 2) for c in range(4)]

        def body(slot, joined):
            middle = [cells[middle_at + c, slot] for c in range(4)]
            above = [cells[middle_at + c, slot + 1] for c in range(4)]
            below = [cells[middle_at + c, slot - 1] for c in range(4)]
            wind_up, wind_down = cells[8, slot + 1], cells[8, slot - 1]
            wind_x, wind_y = cells[9, slot], cells[10, slot]
            loss = SCALE * cells[11, slot]
            seen = []
            for c in range(4):
                total = sign * (flux(wind_up, above, c, 0) - flux(wind_down, below, c, 0))
                along = flux(wind_x, middle, c, 1)
                total += pltpu.roll(along, 15, 0) - pltpu.roll(along, 1, 0)
                along = flux(wind_y, middle, c, 2)
                total += y_change(along, side_y[c], slot, lanes)
                seen.append(jnp.where(groups == slot, pltpu.roll(along, GROUP * slot + DEPTH, 1), joined[c]))
                cells[upper_at + c, slot] = cells[upper_at + c, slot] + factor * total - loss * middle[c]
            return tuple(seen)

        def chunk(i, joined):
            for j in range(CHUNK):
                joined = body(first + CHUNK * i + j, joined)
            return joined

        zeros = tuple(jnp.zeros(tile, jnp.float32) for _ in range(4))
        joined = lax.fori_loop(0, (far - first) // CHUNK, chunk, zeros)
        loss = SCALE * strips[11]
        for c in range(4):
            along = flux(strips[8], side, c, 0)
            total = sign * (pltpu.roll(along, 128 - GROUP, 1) - pltpu.roll(along, GROUP, 1))
            along = flux(strips[9], side, c, 1)
            total += pltpu.roll(along, 15, 0) - pltpu.roll(along, 1, 0)
            total += pltpu.roll(jnp.where(k == DEPTH, joined[c], side_y[c]), 127, 1)
            total -= pltpu.roll(jnp.where(k == DEPTH - 1, joined[c], side_y[c]), 1, 1)
            strips[upper_at + c] = strips[upper_at + c] + side_factor * total - loss * side[c]

    def products(step, middle_at, slot, z):
        return sum(cells[middle_at + c, slot, 0:8, :] * saved[step, c, z] for c in range(4))

    full_step(3, 0, 4)
    for s in range(depth_z):
        z = z_of(s, depth_z)
        prod[z] = products(0, 0, BASE + s, z) + products(1, 4, BASE + s, z)
    full_step(2, 4, 0)
    full_step(1, 0, 4)
    for s in range(depth_z):
        z = z_of(s, depth_z)
        prod[z] = -SCALE * (prod[z] + (products(2, 0, BASE + s, z) + products(3, 4, BASE + s, z)))

    slot_count = table.shape[1]
    level = iota(0, (slot_count, 128)) + 1
    acc[...] = jnp.zeros((slot_count, 128), jnp.float32)

    def by_slot(z, carry):
        total = acc[...]
        for row in range(8):
            cell_slot = jnp.broadcast_to(slots[z, row:row + 1, :], (slot_count, 128))
            term = jnp.broadcast_to(prod[z, row:row + 1, :], (slot_count, 128))
            total = total + jnp.where(cell_slot == level, term, 0.0)
        acc[...] = total
        return carry

    lax.fori_loop(0, depth_z, by_slot, 0)
    slot_terms = jnp.sum(acc[...], axis=1, keepdims=True)
    names = jnp.broadcast_to(table[...], (slot_count, slot_count))
    diagonal = iota(0, (slot_count, slot_count)) == iota(1, (slot_count, slot_count))
    column = jnp.sum(jnp.where(diagonal, names, 0).astype(jnp.float32), axis=1, keepdims=True)
    lane = iota(1, (slot_count, 128))

    def bucket(offset):
        target = jnp.where(lane < FAC_DEV, owner_of(offset) * FAC_DEV + lane, -1).astype(jnp.float32)
        return jnp.sum(jnp.where(column == target, slot_terms, 0.0), axis=0, keepdims=True)

    upward, downward = bucket(1), bucket(-1)
    own[...] = bucket(0)
    even = is_even("gx")
    part_a[...] = jnp.where(even, upward, downward)
    part_b[...] = jnp.where(even, downward, upward)


def last_kernel(cells, strips, out):
    middle_at, upper_at = 4, 0
    depth_z = out.shape[2]
    sign = z_sign()
    lanes = iota(1)
    side = [strips[middle_at + c, 0:8] for c in range(4)]
    side_y = [flux(strips[10, 0:8], side, c, 2) for c in range(4)]

    def body(s):
        slot = BASE + s

        def plane(f, at):
            return cells[f, at, 0:8, :]

        middle = [plane(middle_at + c, slot) for c in range(4)]
        above = [plane(middle_at + c, slot + 1) for c in range(4)]
        below = [plane(middle_at + c, slot - 1) for c in range(4)]
        wide = [cells[middle_at + c, slot] for c in range(4)]
        wind_up, wind_down = plane(8, slot + 1), plane(8, slot - 1)
        wind_x, wind_y = cells[9, slot], plane(10, slot)
        loss = SCALE * plane(11, slot)
        z = z_of(s, depth_z)
        for c in range(4):
            total = sign * (flux(wind_up, above, c, 0) - flux(wind_down, below, c, 0))
            along = flux(wind_x, wide, c, 1)
            total += (pltpu.roll(along, 15, 0) - pltpu.roll(along, 1, 0))[0:8]
            along = flux(wind_y, middle, c, 2)
            total += y_change(along, side_y[c], slot, lanes)
            out[0, c, z] = middle[c]
            out[1, c, z] = plane(upper_at + c, slot) + jnp.float32(0.5 * SCALE) * total - loss * middle[c]

    for s in range(depth_z):
        body(s)


AXES = ("gx", "gy", "gz")


def swap(block, partner):
    counts = tuple(lax.axis_size(axis) for axis in AXES)
    pairs = []
    for place in np.ndindex(*counts):
        other = partner(*place, counts)
        if other is not None:
            pairs.append((int(np.ravel_multi_index(place, counts)), int(np.ravel_multi_index(other, counts))))
    return lax.ppermute(block, AXES, pairs)


def swap_z(x, y, z, counts):
    return x, y, z ^ 1


def swap_xa(x, y, z, counts):
    return x ^ 1, y, z


def swap_xb(x, y, z, counts):
    other = x + 1 if x % 2 else x - 1
    return (other, y, z) if 0 <= other < counts[0] else (x, y ^ 1, z)


def swap_xb_only(x, y, z, counts):
    other = x + 1 if x % 2 else x - 1
    return (other, y, z) if 0 <= other < counts[0] else None


def swap_ring(x, y, z, counts):
    return (x + 1 if x % 2 else x - 1) % counts[0], y, z


def swap_y(side, diagonal):
    def partner(x, y, z, counts):
        other = y ^ 1 if side == 0 else y + 1 if y % 2 else y - 1
        if 0 <= other < counts[1]:
            return x, other, z ^ 1 if diagonal else z
        return x, y, z ^ 1

    return partner


VMEM = pl.BlockSpec(memory_space=pltpu.VMEM)
HBM = pl.BlockSpec(memory_space=pltpu.HBM)


def call(kernel, limit, in_specs, out_shape, scratch=(), aliases=None, cost=None):
    return pl.pallas_call(
        kernel,
        out_shape=[jax.ShapeDtypeStruct(o.shape, o.dtype) for o in out_shape],
        in_specs=in_specs,
        out_specs=[VMEM] * len(out_shape),
        scratch_shapes=list(scratch),
        input_output_aliases=aliases or {},
        compiler_params=pltpu.CompilerParams(vmem_limit_bytes=limit << 20),
        cost_estimate=cost and pl.CostEstimate(flops=cost, bytes_accessed=cost, transcendentals=0),
    )


def in_hbm(array):
    return pltpu.with_memory_space_constraint(array, pltpu.HBM)


def rows_of(count):
    return jax.ShapeDtypeStruct((count, 8, 128), jnp.float32)


def local(adjoint, saved_state, wind_field, facade_slot, facade_table, impedance):
    depth_z = facade_slot.shape[0]
    sides = 1 if lax.axis_size("gy") == 2 else 2
    table = facade_table.reshape(1, -1)
    rates = impedance.reshape(-1, 128)
    adjoint, wind, slots, table, damping, zb, yb, db = call(
        pack_kernel,
        4,
        [HBM] * 5,
        [adjoint, wind_field, facade_slot, table, rows_of(depth_z), rows_of(len(E_PLANES + R_PLANES)), rows_of(Y_ROWS), rows_of(D_ROWS)],
        [pltpu.VMEM(rates.shape, jnp.float32), pltpu.VMEM((8, 128), jnp.int32), pltpu.SemaphoreType.DMA((5,))],
    )(*map(in_hbm, (adjoint, wind_field, facade_slot, table, rates)))
    xa, xb = call(
        pack_x_kernel, 2, [VMEM] * 3, [rows_of(FIELDS * depth_z // 2)] * 2, cost=400000
    )(adjoint, wind, damping)
    saved, = call(fetch_kernel, 1, [HBM], [saved_state], [pltpu.SemaphoreType.DMA], cost=4000000)(in_hbm(saved_state))
    zb = swap(zb, swap_z)
    ds = [swap(db, swap_y(side, True)) for side in range(sides)]
    ys = [swap(yb, swap_y(side, False)) for side in range(sides)]
    xa = swap(xa, swap_xa)
    xb = swap(xb, swap_xb)
    edge_count = (len(E_PLANES) + Y_ROWS + D_ROWS + 1) // 2
    ea, eb = call(
        functools.partial(edge_kernel, sides), 2, [VMEM] * (1 + 2 * sides), [rows_of(edge_count)] * 2
    )(zb, *ys, *ds)
    ea = swap(ea, swap_xa)
    eb = swap(eb, swap_xb_only)
    cells = jax.ShapeDtypeStruct((FIELDS, BASE + depth_z + 1, 16, 128), jnp.float32)
    strips = jax.ShapeDtypeStruct((FIELDS, 16, 128), jnp.float32)
    cells, strips = call(
        functools.partial(fill_kernel, sides), 2, [VMEM] * (6 + 2 * sides), [cells, strips], cost=4000000
    )(adjoint, wind, damping, zb, *ys, *ds, xa, xb)
    row = jax.ShapeDtypeStruct((1, 128), jnp.float32)
    cells, strips, own, part_a, part_b = call(
        step_kernel,
        2,
        [VMEM] * 7,
        [cells, strips, row, row, row],
        [pltpu.VMEM((depth_z, 8, 128), jnp.float32), pltpu.VMEM((table.shape[1], 128), jnp.float32)],
        aliases={0: 0, 1: 1},
    )(cells, strips, ea, eb, saved, slots, table)
    part_b = swap(part_b, swap_ring)
    part_a = swap(part_a, swap_xa)
    out, = call(last_kernel, 2, [VMEM] * 2, [adjoint], cost=4000000)(cells, strips)
    gradient = (own + part_a + part_b)[0, :FAC_DEV]
    return out, gradient


def solution(mesh):
    return jax.shard_map(
        local,
        mesh=mesh,
        in_specs=(
            P(None, None, "gz", "gx", "gy"),
            P(None, None, "gz", "gx", "gy"),
            P(None, "gz", "gx", "gy"),
            P("gz", "gx", "gy"),
            P("gz", "gx", "gy", None),
            P(),
        ),
        out_specs=(P(None, None, "gz", "gx", "gy"), P(("gx", "gy", "gz"))),
        check_vma=False,
    )
```

```python
import functools

import jax
import jax.numpy as jnp
import numpy as np
from jax import lax
from jax.experimental import pallas as pl
from jax.experimental.pallas import tpu as pltpu
from jax.sharding import PartitionSpec as P


FAC_DEV = 32
TIME_STEP = 0.3
SCALE = 2.0 * TIME_STEP

FIELDS = 12
DEPTH = 4
BASE = DEPTH + 1
GROUP = 2 * DEPTH
PASSES = 2
E_PLANES = [(f, t) for t in (1, 2) for f in range(FIELDS)] + [(f, 3) for f in (0, 1, 2, 3, 8, 9)]
R_PLANES = [(f, 3) for f in (4, 5, 6, 7, 10, 11)] + [(f, 4) for f in (0, 1, 2, 3, 8)]
Y_ROWS = FIELDS // 2
D_ROWS = FIELDS // 4


def z_of(s, depth_z):
    return jnp.where(lax.axis_index("gz") == 0, depth_z - 1 - s, s)


def z_sign():
    return jnp.where(lax.axis_index("gz") == 0, jnp.float32(-1.0), jnp.float32(1.0))


def own_planes(depth_z):
    return [(f, s) for f in range(FIELDS) for s in range(depth_z)]


def iota(dim, shape=(8, 128)):
    return lax.broadcasted_iota(jnp.int32, shape, dim)


def is_even(axis):
    return lax.rem(lax.axis_index(axis), 2) == 0


def at_end(axis):
    return (lax.axis_index(axis) == 0) | (lax.axis_index(axis) == lax.axis_size(axis) - 1)


def pack_groups(planes, load):
    groups = iota(1) // GROUP
    row = jnp.zeros((8, 128), jnp.float32)
    for group, plane in planes:
        edge = pltpu.roll(load(*plane), (GROUP * group + DEPTH) % 128, 1)
        row = jnp.where(groups == group, edge, row)
    return row


def unpack_strip(f, y_rows, d_rows):
    lanes = iota(1)
    start = BASE * GROUP
    own = pltpu.roll(y_rows[f // 2], (start - 64 * (f % 2)) % 128, 1)
    beyond = y_shift(d_rows[f // 4], GROUP - 32 * (f % 4))
    return jnp.where(lanes < start, beyond, jnp.where(lanes < start + 64, own, 0.0))


def y_shift(row, shift):
    return pltpu.roll(row, shift % 128, 1) if shift % 128 else row


def merge_sides(parts):
    k = iota(1) % GROUP
    even = is_even("gy")
    if len(parts) == 1:
        start = jnp.where(even, DEPTH, 0)
        return jnp.where((k >= start) & (k < start + DEPTH), parts[0], 0.0)
    second = jnp.where(at_end("gy"), 0.0, parts[1])
    return jnp.where(k >= DEPTH, jnp.where(even, parts[0], second), jnp.where(even, second, parts[0]))


def merged_rows(refs):
    return [merge_sides([ref[i] for ref in refs]) for i in range(refs[0].shape[0])]


def pack_rows(first, second, send_high, rows):
    turned = pltpu.roll(second, 4, 0)
    low = jnp.where(rows < 4, first, turned)
    high = jnp.where(rows < 4, turned, first)
    return jnp.where(send_high, high, low)


def unpack_rows(got_a, got_b, even, rows):
    got_b = jnp.where(at_end("gx"), 0.0, got_b)
    from_high = jnp.where(even, got_a, got_b)
    from_low = jnp.where(even, got_b, got_a)
    first = jnp.where(rows < 4, from_high, from_low)
    second = pltpu.roll(jnp.where(rows < 4, from_low, from_high), 4, 0)
    return first, second


def pack_pairs(planes, xa, xb):
    even = is_even("gx")
    rows = iota(0)
    for i in range(-(-len(planes) // 2)):
        first = planes[2 * i]()
        second = planes[2 * i + 1]() if 2 * i + 1 < len(planes) else first
        xa[i] = pack_rows(first, second, even, rows)
        xb[i] = pack_rows(first, second, jnp.logical_not(even), rows)


def unpack_pairs(xa, xb):
    even = is_even("gx")
    rows = iota(0)
    values = []
    for i in range(xa.shape[0]):
        values += unpack_rows(xa[i], xb[i], even, rows)
    return values


def owner_of(offset):
    count_x, count_y, count_z = (lax.axis_size(a) for a in ("gx", "gy", "gz"))
    x = lax.rem(lax.axis_index("gx") + (offset + count_x), count_x)
    return (x * count_y + lax.axis_index("gy")) * count_z + lax.axis_index("gz")


def loader(adjoint, wind, damping):
    depth_z = damping.shape[0]

    def load(f, s):
        z = z_of(s, depth_z)
        if f < 4:
            return adjoint[1, f, z]
        if f < 8:
            return adjoint[0, f - 4, z]
        if f < 11:
            return wind[f - 8, z]
        return damping[z]

    return load


def pack_kernel(*refs):
    sources = refs[:5]
    adjoint, wind, slots, table, damping, zb, zr, yb, db, impedance, names, sems = refs[5:]
    targets = (adjoint, wind, slots, table, impedance)
    copies = [pltpu.make_async_copy(a, b, sems.at[i]) for i, (a, b) in enumerate(zip(sources, targets))]
    for i in (3, 4, 2, 0, 1):
        copies[i].start()
    depth_z = slots.shape[0]
    names[...] = jnp.zeros((8, 128), jnp.int32)
    copies[3].wait()
    names[:, :table.shape[1]] = jnp.broadcast_to(table[...], (8, table.shape[1]))
    copies[4].wait()
    copies[2].wait()
    ids = names[...]
    local = jnp.zeros((8, 128), jnp.float32)
    for offset in (-1, 0, 1):
        row = owner_of(offset) * FAC_DEV // 128
        values = jnp.broadcast_to(impedance[pl.ds(row, 1), :], (8, 128))
        local = jnp.where(ids // 128 == row, jnp.take_along_axis(values, ids % 128, axis=1), local)
    for z in range(depth_z):
        slot = slots[z]
        found = jnp.take_along_axis(local, jnp.maximum(slot - 1, 0), axis=1)
        damping[z] = jnp.where(slot > 0, found, 0.0)
    copies[0].wait()
    copies[1].wait()
    load = loader(adjoint, wind, damping)
    for ref, planes in ((zb, E_PLANES), (zr, R_PLANES)):
        for i, (f, t) in enumerate(planes):
            ref[i] = load(f, t - 1)
    for i in range(Y_ROWS):
        yb[i] = pack_groups([(8 * j + s, (2 * i + j, s)) for j in range(2) for s in range(depth_z)], load)
    for i in range(D_ROWS):
        db[i] = pack_groups([(4 * j + DEPTH - t, (4 * i + j, t - 1)) for j in range(4) for t in (1, 2, 3)], load)


def pack_x_kernel(adjoint, wind, damping, xa, xb):
    load = loader(adjoint, wind, damping)
    pack_pairs([functools.partial(load, *p) for p in own_planes(damping.shape[0])], xa, xb)


def edge_kernel(sides, zb, *rest):
    y_rows = merged_rows(rest[:sides])
    d_rows = merged_rows(rest[sides:2 * sides])
    planes = [functools.partial(lambda i: zb[i], i) for i in range(len(E_PLANES))]
    planes += [functools.partial(lambda row: row, row) for row in y_rows + d_rows]
    pack_pairs(planes, *rest[2 * sides:])


def coupled(middle, c, k):
    if c == 0:
        return middle[1 + k]
    if c == 1 + k:
        return middle[0]
    return None


def flux(wind, middle, c, k):
    value = wind * middle[c]
    other = coupled(middle, c, k)
    return value if other is None else value + other


def put(cells, f, slot, tx, value):
    cells[f, slot, 8 * tx:8 * tx + 8, :] = value


def fetch_kernel(source, target, sem):
    copy = pltpu.make_async_copy(source, target, sem)
    copy.start()
    copy.wait()


def fill_kernel(sides, adjoint, wind, damping, zb, zr, *rest):
    y_rows = merged_rows(rest[:sides])
    d_rows = merged_rows(rest[sides:2 * sides])
    xa, xb, cells, strips = rest[2 * sides:]
    depth_z = damping.shape[0]
    zero = jnp.zeros((8, 128), jnp.float32)
    load = loader(adjoint, wind, damping)
    planes = own_planes(depth_z)
    for (f, s), value in zip(planes, unpack_pairs(xa, xb)):
        put(cells, f, BASE + s, 0, load(f, s))
        put(cells, f, BASE + s, 1, value)
    for ref, places in ((zb, E_PLANES), (zr, R_PLANES)):
        for i, (f, t) in enumerate(places):
            put(cells, f, BASE - t, 0, ref[i])
    for f in range(FIELDS):
        strips[f, 0:8, :] = unpack_strip(f, y_rows, d_rows)
    for tx in range(2):
        for f in range(9):
            put(cells, f, BASE + depth_z, tx, zero)
        for f in (0, 1, 2, 3, 8):
            put(cells, f, 0, tx, zero)
        for f in (4, 5, 6, 7, 9, 10, 11):
            put(cells, f, 1, tx, zero)
    for f, t in R_PLANES:
        put(cells, f, BASE - t, 1, zero)


def y_change(main, side, slot, lanes):
    above = pltpu.roll(side, 127 - DEPTH - GROUP * slot, 1)
    below = pltpu.roll(side, 129 - DEPTH - GROUP * slot, 1)
    up = jnp.where(lanes == 127, above, pltpu.roll(main, 127, 1))
    return up - jnp.where(lanes == 0, below, pltpu.roll(main, 1, 1))


def step_kernel(cells_in, strips_in, ea, eb, saved, slots, table, cells, strips, own, part_a, part_b, prod, acc):
    del cells_in, strips_in
    depth_z = slots.shape[0]
    far = BASE + depth_z
    edges = unpack_pairs(ea, eb)
    for (f, t), value in zip(E_PLANES, edges):
        put(cells, f, BASE - t, 1, value)
    start = len(E_PLANES)
    for f in range(FIELDS):
        strips[f, 8:16, :] = unpack_strip(f, edges[start:start + Y_ROWS], edges[start + Y_ROWS:])

    tile = (16, 128)
    rows, lanes = iota(0, tile), iota(1, tile)
    groups, k = lanes // GROUP, lanes % GROUP
    x, y = lax.axis_index("gx"), lax.axis_index("gy")
    row_end = jnp.where(x == lax.axis_size("gx") - 1, 8, 12)
    row_restart = jnp.where(x == 0, 16, 12)
    inside = (rows < row_end) | (rows >= row_restart)
    k_first = jnp.where(y == 0, DEPTH, 0)
    k_end = jnp.where(y == lax.axis_size("gy") - 1, DEPTH, GROUP)
    factor = jnp.where(inside, jnp.float32(0.5 * SCALE), 0.0)
    side_factor = jnp.where((k >= k_first) & (k < k_end) & (lanes < GROUP * far), factor, 0.0)
    sign = z_sign()

    def full_step(halo, middle_at, upper_at):
        size = -(-(depth_z + halo) // PASSES)
        first = far - size * PASSES
        side = [strips[middle_at + c] for c in range(4)]
        side_y = [flux(strips[10], side, c, 2) for c in range(4)]

        def body(slot, joined):
            middle = [cells[middle_at + c, slot] for c in range(4)]
            above = [cells[middle_at + c, slot + 1] for c in range(4)]
            below = [cells[middle_at + c, slot - 1] for c in range(4)]
            wind_up, wind_down = cells[8, slot + 1], cells[8, slot - 1]
            wind_x, wind_y = cells[9, slot], cells[10, slot]
            loss = SCALE * cells[11, slot]
            seen = []
            for c in range(4):
                total = sign * (flux(wind_up, above, c, 0) - flux(wind_down, below, c, 0))
                along = flux(wind_x, middle, c, 1)
                total += pltpu.roll(along, 15, 0) - pltpu.roll(along, 1, 0)
                along = flux(wind_y, middle, c, 2)
                total += y_change(along, side_y[c], slot, lanes)
                seen.append(jnp.where(groups == slot, pltpu.roll(along, GROUP * slot + DEPTH, 1), joined[c]))
                cells[upper_at + c, slot] = cells[upper_at + c, slot] + factor * total - loss * middle[c]
            return tuple(seen)

        def chunk(i, joined):
            for j in range(size):
                joined = body(first + size * i + j, joined)
            return joined

        zeros = tuple(jnp.zeros(tile, jnp.float32) for _ in range(4))
        joined = lax.fori_loop(0, PASSES, chunk, zeros)
        loss = SCALE * strips[11]
        for c in range(4):
            along = flux(strips[8], side, c, 0)
            total = sign * (pltpu.roll(along, 128 - GROUP, 1) - pltpu.roll(along, GROUP, 1))
            along = flux(strips[9], side, c, 1)
            total += pltpu.roll(along, 15, 0) - pltpu.roll(along, 1, 0)
            total += pltpu.roll(jnp.where(k == DEPTH, joined[c], side_y[c]), 127, 1)
            total -= pltpu.roll(jnp.where(k == DEPTH - 1, joined[c], side_y[c]), 1, 1)
            strips[upper_at + c] = strips[upper_at + c] + side_factor * total - loss * side[c]

    def products(step, middle_at, slot, z):
        return sum(cells[middle_at + c, slot, 0:8, :] * saved[step, c, z] for c in range(4))

    full_step(3, 0, 4)
    for s in range(depth_z):
        z = z_of(s, depth_z)
        prod[z] = products(0, 0, BASE + s, z) + products(1, 4, BASE + s, z)
    full_step(2, 4, 0)
    full_step(1, 0, 4)
    for s in range(depth_z):
        z = z_of(s, depth_z)
        prod[z] = -SCALE * (prod[z] + (products(2, 0, BASE + s, z) + products(3, 4, BASE + s, z)))

    slot_count = table.shape[1]
    level = iota(0, (slot_count, 128)) + 1
    acc[...] = jnp.zeros((slot_count, 128), jnp.float32)

    def by_slot(i, carry):
        total = acc[...]
        for z in range(4):
            for row in range(8):
                cell_slot = jnp.broadcast_to(slots[4 * i + z, row:row + 1, :], (slot_count, 128))
                term = jnp.broadcast_to(prod[4 * i + z, row:row + 1, :], (slot_count, 128))
                total = total + jnp.where(cell_slot == level, term, 0.0)
        acc[...] = total
        return carry

    lax.fori_loop(0, depth_z // 4, by_slot, 0)
    slot_terms = jnp.sum(acc[...], axis=1, keepdims=True)
    names = jnp.broadcast_to(table[...], (slot_count, slot_count))
    diagonal = iota(0, (slot_count, slot_count)) == iota(1, (slot_count, slot_count))
    column = jnp.sum(jnp.where(diagonal, names, 0).astype(jnp.float32), axis=1, keepdims=True)
    lane = iota(1, (slot_count, 128))

    def bucket(offset):
        target = jnp.where(lane < FAC_DEV, owner_of(offset) * FAC_DEV + lane, -1).astype(jnp.float32)
        return jnp.sum(jnp.where(column == target, slot_terms, 0.0), axis=0, keepdims=True)

    upward, downward = bucket(1), bucket(-1)
    own[...] = bucket(0)
    even = is_even("gx")
    part_a[...] = jnp.where(even, upward, downward)
    part_b[...] = jnp.where(even, downward, upward)


def last_kernel(cells, strips, out):
    middle_at, upper_at = 4, 0
    depth_z = out.shape[2]
    sign = z_sign()
    lanes = iota(1)
    side = [strips[middle_at + c, 0:8] for c in range(4)]
    side_y = [flux(strips[10, 0:8], side, c, 2) for c in range(4)]

    def body(s):
        slot = BASE + s

        def plane(f, at):
            return cells[f, at, 0:8, :]

        middle = [plane(middle_at + c, slot) for c in range(4)]
        above = [plane(middle_at + c, slot + 1) for c in range(4)]
        below = [plane(middle_at + c, slot - 1) for c in range(4)]
        wide = [cells[middle_at + c, slot] for c in range(4)]
        wind_up, wind_down = plane(8, slot + 1), plane(8, slot - 1)
        wind_x, wind_y = cells[9, slot], plane(10, slot)
        loss = SCALE * plane(11, slot)
        z = z_of(s, depth_z)
        for c in range(4):
            total = sign * (flux(wind_up, above, c, 0) - flux(wind_down, below, c, 0))
            along = flux(wind_x, wide, c, 1)
            total += (pltpu.roll(along, 15, 0) - pltpu.roll(along, 1, 0))[0:8]
            along = flux(wind_y, middle, c, 2)
            total += y_change(along, side_y[c], slot, lanes)
            out[0, c, z] = middle[c]
            out[1, c, z] = plane(upper_at + c, slot) + jnp.float32(0.5 * SCALE) * total - loss * middle[c]

    for s in range(depth_z):
        body(s)


AXES = ("gx", "gy", "gz")


def swap(block, partner):
    counts = tuple(lax.axis_size(axis) for axis in AXES)
    pairs = []
    for place in np.ndindex(*counts):
        other = partner(*place, counts)
        if other is not None:
            pairs.append((int(np.ravel_multi_index(place, counts)), int(np.ravel_multi_index(other, counts))))
    return lax.ppermute(block, AXES, pairs)


def swap_z(x, y, z, counts):
    return x, y, z ^ 1


def swap_xa(x, y, z, counts):
    return x ^ 1, y, z


def swap_xb(x, y, z, counts):
    other = x + 1 if x % 2 else x - 1
    return (other, y, z) if 0 <= other < counts[0] else (x, y ^ 1, z)


def swap_xb_only(x, y, z, counts):
    other = x + 1 if x % 2 else x - 1
    return (other, y, z) if 0 <= other < counts[0] else None


def swap_ring(x, y, z, counts):
    return (x + 1 if x % 2 else x - 1) % counts[0], y, z


def swap_y(side, diagonal):
    def partner(x, y, z, counts):
        other = y ^ 1 if side == 0 else y + 1 if y % 2 else y - 1
        if 0 <= other < counts[1]:
            return x, other, z ^ 1 if diagonal else z
        return x, y, z ^ 1

    return partner


VMEM = pl.BlockSpec(memory_space=pltpu.VMEM)
HBM = pl.BlockSpec(memory_space=pltpu.HBM)


def call(kernel, limit, in_specs, out_shape, scratch=(), aliases=None, cost=None):
    return pl.pallas_call(
        kernel,
        out_shape=[jax.ShapeDtypeStruct(o.shape, o.dtype) for o in out_shape],
        in_specs=in_specs,
        out_specs=[VMEM] * len(out_shape),
        scratch_shapes=list(scratch),
        input_output_aliases=aliases or {},
        compiler_params=pltpu.CompilerParams(vmem_limit_bytes=limit << 20),
        cost_estimate=cost and pl.CostEstimate(flops=cost, bytes_accessed=cost, transcendentals=0),
    )


def in_hbm(array):
    return pltpu.with_memory_space_constraint(array, pltpu.HBM)


def rows_of(count):
    return jax.ShapeDtypeStruct((count, 8, 128), jnp.float32)


def local(adjoint, saved_state, wind_field, facade_slot, facade_table, impedance):
    depth_z = facade_slot.shape[0]
    sides = 1 if lax.axis_size("gy") == 2 else 2
    table = facade_table.reshape(1, -1)
    rates = impedance.reshape(-1, 128)
    adjoint, wind, slots, table, damping, zb, zr, yb, db = call(
        pack_kernel,
        4,
        [HBM] * 5,
        [adjoint, wind_field, facade_slot, table, rows_of(depth_z), rows_of(len(E_PLANES)), rows_of(len(R_PLANES)), rows_of(Y_ROWS), rows_of(D_ROWS)],
        [pltpu.VMEM(rates.shape, jnp.float32), pltpu.VMEM((8, 128), jnp.int32), pltpu.SemaphoreType.DMA((5,))],
    )(*map(in_hbm, (adjoint, wind_field, facade_slot, table, rates)))
    xa, xb = call(
        pack_x_kernel, 2, [VMEM] * 3, [rows_of(FIELDS * depth_z // 2)] * 2, cost=400000
    )(adjoint, wind, damping)
    saved, = call(fetch_kernel, 1, [HBM], [saved_state], [pltpu.SemaphoreType.DMA], cost=4000000)(in_hbm(saved_state))
    zb = swap(zb, swap_z)
    zr = swap(zr, swap_z)
    ds = [swap(db, swap_y(side, True)) for side in range(sides)]
    ys = [swap(yb, swap_y(side, False)) for side in range(sides)]
    xa = swap(xa, swap_xa)
    xb = swap(xb, swap_xb)
    edge_count = (len(E_PLANES) + Y_ROWS + D_ROWS + 1) // 2
    ea, eb = call(
        functools.partial(edge_kernel, sides), 2, [VMEM] * (1 + 2 * sides), [rows_of(edge_count)] * 2
    )(zb, *ys, *ds)
    ea = swap(ea, swap_xa)
    eb = swap(eb, swap_xb_only)
    cells = jax.ShapeDtypeStruct((FIELDS, BASE + depth_z + 1, 16, 128), jnp.float32)
    strips = jax.ShapeDtypeStruct((FIELDS, 16, 128), jnp.float32)
    cells, strips = call(
        functools.partial(fill_kernel, sides), 2, [VMEM] * (7 + 2 * sides), [cells, strips], cost=4000000
    )(adjoint, wind, damping, zb, zr, *ys, *ds, xa, xb)
    row = jax.ShapeDtypeStruct((1, 128), jnp.float32)
    cells, strips, own, part_a, part_b = call(
        step_kernel,
        2,
        [VMEM] * 7,
        [cells, strips, row, row, row],
        [pltpu.VMEM((depth_z, 8, 128), jnp.float32), pltpu.VMEM((table.shape[1], 128), jnp.float32)],
        aliases={0: 0, 1: 1},
    )(cells, strips, ea, eb, saved, slots, table)
    part_b = swap(part_b, swap_ring)
    part_a = swap(part_a, swap_xa)
    out, = call(last_kernel, 2, [VMEM] * 2, [adjoint], cost=4000000)(cells, strips)
    gradient = (own + part_a + part_b)[0, :FAC_DEV]
    return out, gradient


def solution(mesh):
    return jax.shard_map(
        local,
        mesh=mesh,
        in_specs=(
            P(None, None, "gz", "gx", "gy"),
            P(None, None, "gz", "gx", "gy"),
            P(None, "gz", "gx", "gy"),
            P("gz", "gx", "gy"),
            P("gz", "gx", "gy", None),
            P(),
        ),
        out_specs=(P(None, None, "gz", "gx", "gy"), P(("gx", "gy", "gz"))),
        check_vma=False,
    )
```

```python
import functools

import jax
import jax.numpy as jnp
import numpy as np
from jax import lax
from jax.experimental import pallas as pl
from jax.experimental.pallas import tpu as pltpu
from jax.sharding import PartitionSpec as P


FAC_DEV = 32
TIME_STEP = 0.3
SCALE = 2.0 * TIME_STEP

FIELDS = 12
DEPTH = 4
BASE = DEPTH + 1
GROUP = 2 * DEPTH
PASSES = 2
E_PLANES = [(f, t) for t in (1, 2) for f in range(FIELDS)] + [(f, 3) for f in (0, 1, 2, 3, 8, 9)]
R_PLANES = [(f, 3) for f in (4, 5, 6, 7, 10, 11)] + [(f, 4) for f in (0, 1, 2, 3, 8)]
Y_ROWS = FIELDS // 2
D_ROWS = FIELDS // 4


def z_of(s, depth_z):
    return jnp.where(lax.axis_index("gz") == 0, depth_z - 1 - s, s)


def z_sign():
    return jnp.where(lax.axis_index("gz") == 0, jnp.float32(-1.0), jnp.float32(1.0))


def own_planes(depth_z):
    return [(f, s) for f in range(FIELDS) for s in range(depth_z)]


def iota(dim, shape=(8, 128)):
    return lax.broadcasted_iota(jnp.int32, shape, dim)


def is_even(axis):
    return lax.rem(lax.axis_index(axis), 2) == 0


def at_end(axis):
    return (lax.axis_index(axis) == 0) | (lax.axis_index(axis) == lax.axis_size(axis) - 1)


def pack_groups(planes, load):
    groups = iota(1) // GROUP
    row = jnp.zeros((8, 128), jnp.float32)
    for group, plane in planes:
        edge = pltpu.roll(load(*plane), (GROUP * group + DEPTH) % 128, 1)
        row = jnp.where(groups == group, edge, row)
    return row


def unpack_strip(f, y_rows, d_rows):
    lanes = iota(1)
    start = BASE * GROUP
    own = pltpu.roll(y_rows[f // 2], (start - 64 * (f % 2)) % 128, 1)
    beyond = y_shift(d_rows[f // 4], GROUP - 32 * (f % 4))
    return jnp.where(lanes < start, beyond, jnp.where(lanes < start + 64, own, 0.0))


def y_shift(row, shift):
    return pltpu.roll(row, shift % 128, 1) if shift % 128 else row


def merge_sides(parts):
    k = iota(1) % GROUP
    even = is_even("gy")
    if len(parts) == 1:
        start = jnp.where(even, DEPTH, 0)
        return jnp.where((k >= start) & (k < start + DEPTH), parts[0], 0.0)
    second = jnp.where(at_end("gy"), 0.0, parts[1])
    return jnp.where(k >= DEPTH, jnp.where(even, parts[0], second), jnp.where(even, second, parts[0]))


def merged_rows(refs):
    return [merge_sides([ref[i] for ref in refs]) for i in range(refs[0].shape[0])]


def pack_rows(first, second, send_high, rows):
    turned = pltpu.roll(second, 4, 0)
    low = jnp.where(rows < 4, first, turned)
    high = jnp.where(rows < 4, turned, first)
    return jnp.where(send_high, high, low)


def unpack_rows(got_a, got_b, even, rows):
    got_b = jnp.where(at_end("gx"), 0.0, got_b)
    from_high = jnp.where(even, got_a, got_b)
    from_low = jnp.where(even, got_b, got_a)
    first = jnp.where(rows < 4, from_high, from_low)
    second = pltpu.roll(jnp.where(rows < 4, from_low, from_high), 4, 0)
    return first, second


def pack_pairs(planes, xa, xb):
    even = is_even("gx")
    rows = iota(0)
    for i in range(-(-len(planes) // 2)):
        first = planes[2 * i]()
        second = planes[2 * i + 1]() if 2 * i + 1 < len(planes) else first
        xa[i] = pack_rows(first, second, even, rows)
        xb[i] = pack_rows(first, second, jnp.logical_not(even), rows)


def unpack_pairs(xa, xb):
    even = is_even("gx")
    rows = iota(0)
    values = []
    for i in range(xa.shape[0]):
        values += unpack_rows(xa[i], xb[i], even, rows)
    return values


def owner_of(offset):
    count_x, count_y, count_z = (lax.axis_size(a) for a in ("gx", "gy", "gz"))
    x = lax.rem(lax.axis_index("gx") + (offset + count_x), count_x)
    return (x * count_y + lax.axis_index("gy")) * count_z + lax.axis_index("gz")


def loader(adjoint, wind, damping):
    depth_z = damping.shape[0]

    def load(f, s):
        z = z_of(s, depth_z)
        if f < 4:
            return adjoint[1, f, z]
        if f < 8:
            return adjoint[0, f - 4, z]
        if f < 11:
            return wind[f - 8, z]
        return damping[z]

    return load


def pack_kernel(*refs):
    sources = refs[:5]
    adjoint, wind, slots, table, damping, zb, zr, yb, db, impedance, names, sems = refs[5:]
    targets = (adjoint, wind, slots, table, impedance)
    copies = [pltpu.make_async_copy(a, b, sems.at[i]) for i, (a, b) in enumerate(zip(sources, targets))]
    for i in (3, 4, 2, 0, 1):
        copies[i].start()
    depth_z = slots.shape[0]
    names[...] = jnp.zeros((8, 128), jnp.int32)
    copies[3].wait()
    names[:, :table.shape[1]] = jnp.broadcast_to(table[...], (8, table.shape[1]))
    copies[4].wait()
    copies[2].wait()
    ids = names[...]
    local = jnp.zeros((8, 128), jnp.float32)
    for offset in (-1, 0, 1):
        row = owner_of(offset) * FAC_DEV // 128
        values = jnp.broadcast_to(impedance[pl.ds(row, 1), :], (8, 128))
        local = jnp.where(ids // 128 == row, jnp.take_along_axis(values, ids % 128, axis=1), local)
    for z in range(depth_z):
        slot = slots[z]
        found = jnp.take_along_axis(local, jnp.maximum(slot - 1, 0), axis=1)
        damping[z] = jnp.where(slot > 0, found, 0.0)
    copies[0].wait()
    copies[1].wait()
    load = loader(adjoint, wind, damping)
    for ref, planes in ((zb, E_PLANES), (zr, R_PLANES)):
        for i, (f, t) in enumerate(planes):
            ref[i] = load(f, t - 1)
    for i in range(Y_ROWS):
        yb[i] = pack_groups([(8 * j + s, (2 * i + j, s)) for j in range(2) for s in range(depth_z)], load)
    for i in range(D_ROWS):
        db[i] = pack_groups([(4 * j + DEPTH - t, (4 * i + j, t - 1)) for j in range(4) for t in (1, 2, 3)], load)


def pack_x_kernel(adjoint, wind, damping, xa, xb):
    load = loader(adjoint, wind, damping)
    pack_pairs([functools.partial(load, *p) for p in own_planes(damping.shape[0])], xa, xb)


def edge_kernel(sides, zb, *rest):
    y_rows = merged_rows(rest[:sides])
    d_rows = merged_rows(rest[sides:2 * sides])
    planes = [functools.partial(lambda i: zb[i], i) for i in range(len(E_PLANES))]
    planes += [functools.partial(lambda row: row, row) for row in y_rows + d_rows]
    pack_pairs(planes, *rest[2 * sides:])


def coupled(middle, c, k):
    if c == 0:
        return middle[1 + k]
    if c == 1 + k:
        return middle[0]
    return None


def flux(wind, middle, c, k):
    value = wind * middle[c]
    other = coupled(middle, c, k)
    return value if other is None else value + other


def put(cells, f, slot, tx, value):
    cells[f, slot, 8 * tx:8 * tx + 8, :] = value


def y_change(main, side, slot, lanes):
    above = pltpu.roll(side, 127 - DEPTH - GROUP * slot, 1)
    below = pltpu.roll(side, 129 - DEPTH - GROUP * slot, 1)
    up = jnp.where(lanes == 127, above, pltpu.roll(main, 127, 1))
    return up - jnp.where(lanes == 0, below, pltpu.roll(main, 1, 1))


def cell_factor():
    rows = iota(0, (16, 128))
    x = lax.axis_index("gx")
    row_end = jnp.where(x == lax.axis_size("gx") - 1, 8, 12)
    row_restart = jnp.where(x == 0, 16, 12)
    return jnp.where((rows < row_end) | (rows >= row_restart), jnp.float32(0.5 * SCALE), 0.0)


def side_fluxes(strips, middle_at):
    side = [strips[middle_at + c] for c in range(4)]
    return side, [flux(strips[10], side, c, 2) for c in range(4)]


def step_layers(cells, first, size, passes, middle_at, upper_at, side_y, joined):
    lanes = iota(1, (16, 128))
    groups = lanes // GROUP
    factor = cell_factor()
    sign = z_sign()

    def body(slot, joined):
        middle = [cells[middle_at + c, slot] for c in range(4)]
        above = [cells[middle_at + c, slot + 1] for c in range(4)]
        below = [cells[middle_at + c, slot - 1] for c in range(4)]
        wind_up, wind_down = cells[8, slot + 1], cells[8, slot - 1]
        wind_x, wind_y = cells[9, slot], cells[10, slot]
        loss = SCALE * cells[11, slot]
        seen = []
        for c in range(4):
            total = sign * (flux(wind_up, above, c, 0) - flux(wind_down, below, c, 0))
            along = flux(wind_x, middle, c, 1)
            total += pltpu.roll(along, 15, 0) - pltpu.roll(along, 1, 0)
            along = flux(wind_y, middle, c, 2)
            total += y_change(along, side_y[c], slot, lanes)
            seen.append(jnp.where(groups == slot, pltpu.roll(along, GROUP * slot + DEPTH, 1), joined[c]))
            cells[upper_at + c, slot] = cells[upper_at + c, slot] + factor * total - loss * middle[c]
        return tuple(seen)

    def some(i, joined):
        for j in range(size):
            joined = body(first + size * i + j, joined)
        return joined

    return lax.fori_loop(0, passes, some, joined) if passes > 1 else some(0, joined)


def no_edges():
    return tuple(jnp.zeros((16, 128), jnp.float32) for _ in range(4))


def fetch_kernel(source, target, sem):
    copy = pltpu.make_async_copy(source, target, sem)
    copy.start()
    copy.wait()


def fill_kernel(sides, adjoint, wind, damping, zb, zr, *rest):
    y_rows = merged_rows(rest[:sides])
    d_rows = merged_rows(rest[sides:2 * sides])
    xa, xb, cells, strips, joined = rest[2 * sides:]
    depth_z = damping.shape[0]
    zero = jnp.zeros((8, 128), jnp.float32)
    load = loader(adjoint, wind, damping)
    planes = own_planes(depth_z)
    for (f, s), value in zip(planes, unpack_pairs(xa, xb)):
        put(cells, f, BASE + s, 0, load(f, s))
        put(cells, f, BASE + s, 1, value)
    for ref, places in ((zb, E_PLANES), (zr, R_PLANES)):
        for i, (f, t) in enumerate(places):
            put(cells, f, BASE - t, 0, ref[i])
    for f in range(FIELDS):
        strips[f, 0:8, :] = unpack_strip(f, y_rows, d_rows)
    for tx in range(2):
        for f in range(9):
            put(cells, f, BASE + depth_z, tx, zero)
        for f in (0, 1, 2, 3, 8):
            put(cells, f, 0, tx, zero)
        for f in (4, 5, 6, 7, 9, 10, 11):
            put(cells, f, 1, tx, zero)
    for f, t in R_PLANES:
        put(cells, f, BASE - t, 1, zero)
    for f in (0, 1, 2, 3, 10):
        strips[f, 8:16, :] = zero
    _, side_y = side_fluxes(strips, 0)
    for c, value in enumerate(step_layers(cells, BASE + 1, depth_z - 1, 1, 0, 4, side_y, no_edges())):
        joined[c] = value


def step_kernel(cells_in, strips_in, early, ea, eb, saved, slots, table, cells, strips, own, part_a, part_b, prod, acc):
    del cells_in, strips_in
    depth_z = slots.shape[0]
    far = BASE + depth_z
    edges = unpack_pairs(ea, eb)
    for (f, t), value in zip(E_PLANES, edges):
        put(cells, f, BASE - t, 1, value)
    start = len(E_PLANES)
    for f in range(FIELDS):
        strips[f, 8:16, :] = unpack_strip(f, edges[start:start + Y_ROWS], edges[start + Y_ROWS:])

    tile = (16, 128)
    lanes = iota(1, tile)
    k = lanes % GROUP
    y = lax.axis_index("gy")
    k_first = jnp.where(y == 0, DEPTH, 0)
    k_end = jnp.where(y == lax.axis_size("gy") - 1, DEPTH, GROUP)
    factor = cell_factor()
    side_factor = jnp.where((k >= k_first) & (k < k_end) & (lanes < GROUP * far), factor, 0.0)
    sign = z_sign()

    def full_step(halo, middle_at, upper_at):
        side, side_y = side_fluxes(strips, middle_at)
        if halo == DEPTH - 1:
            joined = tuple(early[c] for c in range(4))
            joined = step_layers(cells, BASE - halo, halo + 1, 1, middle_at, upper_at, side_y, joined)
            edge_factor = factor[8:16]
            for slot in range(BASE + 1, far):
                for c in range(4):
                    extra = y_change(jnp.zeros((8, 128), jnp.float32), side_y[c][8:16], slot, lanes[8:16])
                    cells[upper_at + c, slot, 8:16, :] = cells[upper_at + c, slot, 8:16, :] + edge_factor * extra
        else:
            size = -(-(depth_z + halo) // PASSES)
            first = far - size * PASSES
            joined = step_layers(cells, first, size, PASSES, middle_at, upper_at, side_y, no_edges())
        loss = SCALE * strips[11]
        for c in range(4):
            along = flux(strips[8], side, c, 0)
            total = sign * (pltpu.roll(along, 128 - GROUP, 1) - pltpu.roll(along, GROUP, 1))
            along = flux(strips[9], side, c, 1)
            total += pltpu.roll(along, 15, 0) - pltpu.roll(along, 1, 0)
            total += pltpu.roll(jnp.where(k == DEPTH, joined[c], side_y[c]), 127, 1)
            total -= pltpu.roll(jnp.where(k == DEPTH - 1, joined[c], side_y[c]), 1, 1)
            strips[upper_at + c] = strips[upper_at + c] + side_factor * total - loss * side[c]

    def products(step, middle_at, slot, z):
        return sum(cells[middle_at + c, slot, 0:8, :] * saved[step, c, z] for c in range(4))

    full_step(3, 0, 4)
    for s in range(depth_z):
        z = z_of(s, depth_z)
        prod[z] = products(0, 0, BASE + s, z) + products(1, 4, BASE + s, z)
    full_step(2, 4, 0)
    full_step(1, 0, 4)
    for s in range(depth_z):
        z = z_of(s, depth_z)
        prod[z] = -SCALE * (prod[z] + (products(2, 0, BASE + s, z) + products(3, 4, BASE + s, z)))

    slot_count = table.shape[1]
    level = iota(0, (slot_count, 128)) + 1
    acc[...] = jnp.zeros((slot_count, 128), jnp.float32)

    def by_slot(i, carry):
        total = acc[...]
        for z in range(4):
            for row in range(8):
                cell_slot = jnp.broadcast_to(slots[4 * i + z, row:row + 1, :], (slot_count, 128))
                term = jnp.broadcast_to(prod[4 * i + z, row:row + 1, :], (slot_count, 128))
                total = total + jnp.where(cell_slot == level, term, 0.0)
        acc[...] = total
        return carry

    lax.fori_loop(0, depth_z // 4, by_slot, 0)
    slot_terms = jnp.sum(acc[...], axis=1, keepdims=True)
    names = jnp.broadcast_to(table[...], (slot_count, slot_count))
    diagonal = iota(0, (slot_count, slot_count)) == iota(1, (slot_count, slot_count))
    column = jnp.sum(jnp.where(diagonal, names, 0).astype(jnp.float32), axis=1, keepdims=True)
    lane = iota(1, (slot_count, 128))

    def bucket(offset):
        target = jnp.where(lane < FAC_DEV, owner_of(offset) * FAC_DEV + lane, -1).astype(jnp.float32)
        return jnp.sum(jnp.where(column == target, slot_terms, 0.0), axis=0, keepdims=True)

    upward, downward = bucket(1), bucket(-1)
    own[...] = bucket(0)
    even = is_even("gx")
    part_a[...] = jnp.where(even, upward, downward)
    part_b[...] = jnp.where(even, downward, upward)


def last_kernel(cells, strips, out):
    middle_at, upper_at = 4, 0
    depth_z = out.shape[2]
    sign = z_sign()
    lanes = iota(1)
    side = [strips[middle_at + c, 0:8] for c in range(4)]
    side_y = [flux(strips[10, 0:8], side, c, 2) for c in range(4)]

    def body(s):
        slot = BASE + s

        def plane(f, at):
            return cells[f, at, 0:8, :]

        middle = [plane(middle_at + c, slot) for c in range(4)]
        above = [plane(middle_at + c, slot + 1) for c in range(4)]
        below = [plane(middle_at + c, slot - 1) for c in range(4)]
        wide = [cells[middle_at + c, slot] for c in range(4)]
        wind_up, wind_down = plane(8, slot + 1), plane(8, slot - 1)
        wind_x, wind_y = cells[9, slot], plane(10, slot)
        loss = SCALE * plane(11, slot)
        z = z_of(s, depth_z)
        for c in range(4):
            total = sign * (flux(wind_up, above, c, 0) - flux(wind_down, below, c, 0))
            along = flux(wind_x, wide, c, 1)
            total += (pltpu.roll(along, 15, 0) - pltpu.roll(along, 1, 0))[0:8]
            along = flux(wind_y, middle, c, 2)
            total += y_change(along, side_y[c], slot, lanes)
            out[0, c, z] = middle[c]
            out[1, c, z] = plane(upper_at + c, slot) + jnp.float32(0.5 * SCALE) * total - loss * middle[c]

    for s in range(depth_z):
        body(s)


AXES = ("gx", "gy", "gz")


def swap(block, partner):
    counts = tuple(lax.axis_size(axis) for axis in AXES)
    pairs = []
    for place in np.ndindex(*counts):
        other = partner(*place, counts)
        if other is not None:
            pairs.append((int(np.ravel_multi_index(place, counts)), int(np.ravel_multi_index(other, counts))))
    return lax.ppermute(block, AXES, pairs)


def swap_z(x, y, z, counts):
    return x, y, z ^ 1


def swap_xa(x, y, z, counts):
    return x ^ 1, y, z


def swap_xb(x, y, z, counts):
    other = x + 1 if x % 2 else x - 1
    return (other, y, z) if 0 <= other < counts[0] else (x, y ^ 1, z)


def swap_xb_only(x, y, z, counts):
    other = x + 1 if x % 2 else x - 1
    return (other, y, z) if 0 <= other < counts[0] else None


def swap_ring(x, y, z, counts):
    return (x + 1 if x % 2 else x - 1) % counts[0], y, z


def swap_y(side, diagonal):
    def partner(x, y, z, counts):
        other = y ^ 1 if side == 0 else y + 1 if y % 2 else y - 1
        if 0 <= other < counts[1]:
            return x, other, z ^ 1 if diagonal else z
        return x, y, z ^ 1

    return partner


VMEM = pl.BlockSpec(memory_space=pltpu.VMEM)
HBM = pl.BlockSpec(memory_space=pltpu.HBM)


def call(kernel, limit, in_specs, out_shape, scratch=(), aliases=None, cost=None):
    return pl.pallas_call(
        kernel,
        out_shape=[jax.ShapeDtypeStruct(o.shape, o.dtype) for o in out_shape],
        in_specs=in_specs,
        out_specs=[VMEM] * len(out_shape),
        scratch_shapes=list(scratch),
        input_output_aliases=aliases or {},
        compiler_params=pltpu.CompilerParams(vmem_limit_bytes=limit << 20),
        cost_estimate=cost and pl.CostEstimate(flops=cost, bytes_accessed=cost, transcendentals=0),
    )


def in_hbm(array):
    return pltpu.with_memory_space_constraint(array, pltpu.HBM)


def rows_of(count):
    return jax.ShapeDtypeStruct((count, 8, 128), jnp.float32)


def local(adjoint, saved_state, wind_field, facade_slot, facade_table, impedance):
    depth_z = facade_slot.shape[0]
    sides = 1 if lax.axis_size("gy") == 2 else 2
    table = facade_table.reshape(1, -1)
    rates = impedance.reshape(-1, 128)
    adjoint, wind, slots, table, damping, zb, zr, yb, db = call(
        pack_kernel,
        4,
        [HBM] * 5,
        [adjoint, wind_field, facade_slot, table, rows_of(depth_z), rows_of(len(E_PLANES)), rows_of(len(R_PLANES)), rows_of(Y_ROWS), rows_of(D_ROWS)],
        [pltpu.VMEM(rates.shape, jnp.float32), pltpu.VMEM((8, 128), jnp.int32), pltpu.SemaphoreType.DMA((5,))],
    )(*map(in_hbm, (adjoint, wind_field, facade_slot, table, rates)))
    xa, xb = call(
        pack_x_kernel, 2, [VMEM] * 3, [rows_of(FIELDS * depth_z // 2)] * 2, cost=400000
    )(adjoint, wind, damping)
    saved, = call(fetch_kernel, 1, [HBM], [saved_state], [pltpu.SemaphoreType.DMA], cost=4000000)(in_hbm(saved_state))
    zb = swap(zb, swap_z)
    zr = swap(zr, swap_z)
    ds = [swap(db, swap_y(side, True)) for side in range(sides)]
    ys = [swap(yb, swap_y(side, False)) for side in range(sides)]
    xa = swap(xa, swap_xa)
    xb = swap(xb, swap_xb)
    edge_count = (len(E_PLANES) + Y_ROWS + D_ROWS + 1) // 2
    ea, eb = call(
        functools.partial(edge_kernel, sides), 2, [VMEM] * (1 + 2 * sides), [rows_of(edge_count)] * 2
    )(zb, *ys, *ds)
    ea = swap(ea, swap_xa)
    eb = swap(eb, swap_xb_only)
    cells = jax.ShapeDtypeStruct((FIELDS, BASE + depth_z + 1, 16, 128), jnp.float32)
    strips = jax.ShapeDtypeStruct((FIELDS, 16, 128), jnp.float32)
    cells, strips, early = call(
        functools.partial(fill_kernel, sides),
        2,
        [VMEM] * (7 + 2 * sides),
        [cells, strips, jax.ShapeDtypeStruct((4, 16, 128), jnp.float32)],
        cost=4000000,
    )(adjoint, wind, damping, zb, zr, *ys, *ds, xa, xb)
    row = jax.ShapeDtypeStruct((1, 128), jnp.float32)
    cells, strips, own, part_a, part_b = call(
        step_kernel,
        2,
        [VMEM] * 8,
        [cells, strips, row, row, row],
        [pltpu.VMEM((depth_z, 8, 128), jnp.float32), pltpu.VMEM((table.shape[1], 128), jnp.float32)],
        aliases={0: 0, 1: 1},
    )(cells, strips, early, ea, eb, saved, slots, table)
    part_b = swap(part_b, swap_ring)
    part_a = swap(part_a, swap_xa)
    out, = call(last_kernel, 2, [VMEM] * 2, [adjoint], cost=4000000)(cells, strips)
    gradient = (own + part_a + part_b)[0, :FAC_DEV]
    return out, gradient


def solution(mesh):
    return jax.shard_map(
        local,
        mesh=mesh,
        in_specs=(
            P(None, None, "gz", "gx", "gy"),
            P(None, None, "gz", "gx", "gy"),
            P(None, "gz", "gx", "gy"),
            P("gz", "gx", "gy"),
            P("gz", "gx", "gy", None),
            P(),
        ),
        out_specs=(P(None, None, "gz", "gx", "gy"), P(("gx", "gy", "gz"))),
        check_vma=False,
    )
```
